32 devices in a mesh: grp: 2 (over x), seq: 16 (over z, y, core).
Axes of the slice: x: 2, y: 2, z: 4, core: 2. Of those that a mesh axis runs over, the one named last changes fastest.
Arguments:
- query_rows: bfloat16 [16384, 1536], P(('grp', 'seq')), parts along dimension 0, may hold values from -6 to 6
- key_rows: bfloat16 [16384, 1536], P(('grp', 'seq')), parts along dimension 0, may hold values from -6 to 6
- value_rows: bfloat16 [16384, 1536], P(('grp', 'seq')), parts along dimension 0, may hold values from -6 to 6
- doc_start: int32 [16384], P(('grp', 'seq')), parts along dimension 0, may hold values from 0 to 8191, as said below
Outputs:
- attention_out: bfloat16 [16384, 1536], P(('grp', 'seq')), parts along dimension 0
The draws below stay inside these ranges and needn't reach their ends.
There are 2 independent parts, one for each index of `grp`. The reference program is written for one: setup_inputs(seed, part) draws one part's arguments, and reference() takes and returns one part's arrays. A program takes and returns all parts, laid end to end along the dimension named above; each array names one. Nothing has to cross between parts.
Inputs may be any that keep to these rules, and one draw needn't show every extreme that they name: `doc_start`: the position of the first token of the token's document: never falling, equal to the token's own position at a document's first token and constant up to the next one.
All inputs are finite; a program needn't handle non-finite values.
Results may differ from the reference program's by a relative error of at most 0.0038.
Values may be sent and summed in bfloat16 or wider, within the bound.
A program may use at most 64 MiB of HBM per device.

```python
import math
import jax
import jax.numpy as jnp
from jax import lax

AH = 12
DH = 128
WINDOW = 2048
TOK_DEV = 512
TOKENS = 8192


def paired_rows(key):
    width = AH * DH
    query_base = jnp.clip(jax.random.normal(jax.random.fold_in(key, 11), (TOKENS, width), jnp.float32), -6.0, 6.0)
    key_base = jnp.clip(jax.random.normal(jax.random.fold_in(key, 12), (TOKENS, width), jnp.float32), -6.0, 6.0)
    return (query_base, key_base)


def draw_query_rows(key, part):
    return paired_rows(key)[0].astype(jnp.bfloat16)


def draw_key_rows(key, part):
    return paired_rows(key)[1].astype(jnp.bfloat16)


def draw_doc_start(key, part):
    shortest = 2 * TOK_DEV
    longest = min(64 * TOK_DEV, TOKENS // 2)
    doc_count = TOKENS // shortest + 1
    lengths = jax.random.randint(key, (doc_count,), shortest, longest + 1, dtype=jnp.int32)
    finish = jnp.cumsum(lengths).astype(jnp.int32)
    begins = finish - lengths
    places = jnp.arange(TOKENS, dtype=jnp.int32)
    which = jnp.searchsorted(finish, places, side='right')
    return begins[which].astype(jnp.int32)


def levels(key, extent, cuts, low, top_value):
    def one(axis_at, blocks):
        draws = jax.random.uniform(jax.random.fold_in(jax.random.fold_in(key, 6), axis_at), (blocks,), jnp.float32, low / len(cuts), top_value / len(cuts))
        return jnp.repeat(jnp.exp(draws), extent[axis_at] // blocks).reshape((-1,) + (1,) * (len(extent) - axis_at - 1))

    factor_of = one(*cuts[0])
    for cut in cuts[1:]:
        factor_of = factor_of * one(*cut)
    return factor_of


def bell_draw(own_key, extent, deviation, limit, cuts=(), kind=jnp.bfloat16):
    array = deviation * jax.random.normal(own_key, extent, jnp.float32)
    if cuts:
        array = array * levels(own_key, extent, cuts, -0.22, 0.18)
    return jnp.clip(array, -limit, limit).astype(kind)


def setup_inputs(seed: int = 0, part: int = 0) -> dict:
    seeds = jax.random.split(jax.random.key(seed), 5)
    own_keys = jax.random.split(jax.random.fold_in(seeds[4], part), 5)
    return {
        "query_rows": draw_query_rows(jax.random.fold_in(jax.random.fold_in(seeds[4], part), 71), part),
        "key_rows": draw_key_rows(jax.random.fold_in(jax.random.fold_in(seeds[4], part), 71), part),
        "value_rows": bell_draw(own_keys[2], (TOKENS, AH * DH), 1.0, 6.0, ((0, 16),)),
        "doc_start": draw_doc_start(jax.random.fold_in(jax.random.fold_in(seeds[4], part), 71), part),
    }


def attention_block(block_index, query_rows, padded_keys, padded_values, doc_start):
    first_row = (block_index * TOK_DEV).astype(jnp.int32)
    queries_here = lax.dynamic_slice_in_dim(query_rows, first_row, TOK_DEV, 0)
    keys_here = lax.dynamic_slice_in_dim(padded_keys, first_row, WINDOW + TOK_DEV, 0)
    values_here = lax.dynamic_slice_in_dim(padded_values, first_row, WINDOW + TOK_DEV, 0)
    starts = lax.dynamic_slice_in_dim(doc_start, first_row, TOK_DEV, 0)
    query_place = first_row + jnp.arange(TOK_DEV, dtype=jnp.int32)
    key_place = first_row - WINDOW + jnp.arange(WINDOW + TOK_DEV, dtype=jnp.int32)
    allowed = (key_place[None, :] <= query_place[:, None]) & (key_place[None, :] > query_place[:, None] - WINDOW) & (key_place[None, :] >= starts[:, None])
    query_heads = queries_here.reshape(TOK_DEV, AH, DH).astype(jnp.float32)
    key_heads = keys_here.reshape(WINDOW + TOK_DEV, AH, DH).astype(jnp.float32)
    value_heads = values_here.reshape(WINDOW + TOK_DEV, AH, DH).astype(jnp.float32)
    scores = jnp.einsum('qhd,khd->hqk', query_heads, key_heads) * (1.0 / math.sqrt(DH))
    scores = jnp.where(allowed[None], scores, -jnp.inf)
    largest = lax.optimization_barrier(jnp.max(scores, axis=2, keepdims=True))
    powers = jnp.exp(scores - largest)
    totals = lax.optimization_barrier(jnp.sum(powers, axis=2, keepdims=True))
    weights = powers.astype(jnp.bfloat16)
    mixed = jnp.einsum('hqk,khd->hqd', weights.astype(jnp.float32), value_heads) / totals
    return mixed.transpose(1, 0, 2).reshape(TOK_DEV, AH * DH).astype(jnp.bfloat16)

def reference(query_rows, key_rows, value_rows, doc_start):
    padding = jnp.zeros((WINDOW, AH * DH), key_rows.dtype)
    padded_keys = jnp.concatenate([padding, key_rows], axis=0)
    padded_values = jnp.concatenate([padding, value_rows], axis=0)
    blocks = jnp.arange(TOKENS // TOK_DEV, dtype=jnp.int32)
    attention_out = lax.map(lambda number: attention_block(number, query_rows, padded_keys, padded_values, doc_start), blocks)
    return attention_out.reshape(TOKENS, AH * DH)
```

```python
import functools
import math

import jax
import jax.numpy as jnp
from jax import lax
from jax.experimental import pallas as pl
from jax.experimental.pallas import tpu as pltpu
from jax.sharding import PartitionSpec as P

AH = 12
DH = 128
WINDOW = 2048
MESH = pl.DeviceIdType.MESH
HIDDEN = -1e30
AHEAD = 3
PIECES = (1, 1, 1, 1)


def kernel(n, rows, doc_hbm, q_hbm, k_hbm, v_hbm, out_ref,
           q_buf, k_buf, v_buf, doc_ref, low, top_buf, sum_buf, mix_buf, own_sem, doc_sem, send_sem, recv_sem):
    group = lax.axis_index("grp")
    me = lax.axis_index("seq")
    upper = (me // 2) % 2
    odd = me % 2
    beside = me + 2 - 4 * upper
    twin = me + 1 - 2 * odd
    half = rows // 2
    sources = (k_hbm, v_hbm)
    buffers = (k_buf, v_buf)

    def columns(ref, head, first, count):
        return ref.at[pl.ds(first, count), pl.ds(pl.multiple_of(head * DH, DH), DH)]

    def slot(which, head, shard, first, count):
        return buffers[which].at[head, pl.ds(shard * rows + first, count), :]

    def own_copies(head):
        pairs = [(q_hbm, q_buf.at[head])] + [(sources[w], slot(w, head, 4, 0, rows)) for w in (0, 1)]
        return [
            pltpu.make_async_copy(columns(source, head, 0, rows), target, own_sem.at[at, head])
            for at, (source, target) in enumerate(pairs)
        ]

    landing = (0, 2, 3, 1)

    def copies(kind, head, source_shard, target, which=(0, 1), pieces=None):
        made = []
        count = rows // PIECES[kind]
        for w in which:
            for piece in range(PIECES[kind]) if pieces is None else pieces:
                if source_shard is None:
                    source = columns(sources[w], head, piece * count, count)
                else:
                    source = slot(w, head, source_shard, piece * count, count)
                made.append(pltpu.make_async_remote_copy(
                    src_ref=source,
                    dst_ref=slot(w, head, landing[kind], piece * count, count),
                    send_sem=send_sem.at[kind, w, piece, head],
                    recv_sem=recv_sem.at[kind, w, piece, head],
                    device_id=(group, target),
                    device_id_type=MESH,
                ))
        return made

    def begin(condition, kind, head, source_shard, target, which=(0, 1), pieces=None):
        @pl.when(condition)
        def _():
            for copy in copies(kind, head, source_shard, target, which, pieces):
                copy.start()

    def arrived(kind, head, condition, which=(0, 1), pieces=None):
        @pl.when(condition)
        def _():
            for copy in copies(kind, head, None, twin, which, pieces):
                copy.wait_recv()

    def gone(kind, head, condition):
        @pl.when(condition)
        def _():
            for copy in copies(kind, head, None, twin):
                copy.wait_send()

    def send_own(head):
        begin(me + 4 < n, 0, head, None, me + 4)
        begin(upper == 0, 1, head, None, beside)

    doc_copy = pltpu.make_async_copy(doc_hbm, doc_ref, doc_sem)
    doc_copy.start()
    barrier = pltpu.get_barrier_semaphore()
    pl.semaphore_signal(barrier, inc=1, device_id=(group, beside), device_id_type=MESH)
    pl.semaphore_signal(barrier, inc=1, device_id=(group, twin), device_id_type=MESH)

    @pl.when(me >= 4)
    def _():
        pl.semaphore_signal(barrier, inc=1, device_id=(group, me - 4), device_id_type=MESH)

    @pl.when(me + 4 < n)
    def _():
        pl.semaphore_signal(barrier, inc=1, device_id=(group, me + 4), device_id_type=MESH)

    peers = 2 + (me >= 4).astype(jnp.int32) + (me + 4 < n).astype(jnp.int32)
    pl.semaphore_wait(barrier, peers)

    for head in range(AHEAD):
        send_own(head)

    def first(head, carry):
        begin(odd == 0, 2, head, None, twin)
        return carry

    lax.fori_loop(0, AH, first, 0)

    def fetch(head, carry):
        for copy in own_copies(head):
            copy.start()
        return carry

    lax.fori_loop(0, AH, fetch, 0)

    for shard in range(4):
        @pl.when(me < 4 - shard)
        def _():
            def clear(head, carry):
                for buffer in buffers:
                    buffer[head, pl.ds(shard * rows, rows), :] = jnp.zeros((rows, DH), jnp.bfloat16)
                return carry

            lax.fori_loop(0, AH, clear, 0)

    doc_copy.wait()
    row = lax.broadcasted_iota(jnp.int32, (rows, DH), 0)
    starts = jnp.transpose(jnp.broadcast_to(doc_ref[...], (DH, rows)))
    low[...] = jnp.maximum(starts - (me * rows - WINDOW), row + 1)

    scale = math.log2(math.e) / math.sqrt(DH)

    def absorb(state, part, head, spans):
        span = slice(part * half, (part + 1) * half)
        queries = q_buf[head, span, :]
        lowest = low[span, 0:1]
        every = []
        for start, count in spans:
            scores = lax.dot_general(
                queries, k_buf[head, start:start + count, :], (((1,), (1,)), ((), ())),
                preferred_element_type=jnp.float32,
            )
            place = start + lax.broadcasted_iota(jnp.int32, (half, count), 1)
            allowed = place >= lowest
            if start >= WINDOW:
                query = part * half + lax.broadcasted_iota(jnp.int32, (half, count), 0)
                allowed = allowed & (place <= query + WINDOW)
            every.append(jnp.where(allowed, scores, HIDDEN))
        largest = functools.reduce(jnp.maximum, [jnp.max(x, axis=1, keepdims=True) for x in every])
        if state is not None:
            largest = jnp.maximum(largest, state[0])
        total = mixed = 0.0
        if state is not None:
            fade = jnp.exp2((state[0] - largest) * scale)
            total, mixed = state[1] * fade, state[2] * fade
        for (start, count), scores in zip(spans, every):
            powers = jnp.exp2((scores - largest) * scale)
            total = total + jnp.sum(powers, axis=1, keepdims=True)
            mixed = mixed + jnp.dot(
                powers.astype(jnp.bfloat16), v_buf[head, start:start + count, :],
                preferred_element_type=jnp.float32,
            )
        return largest, total, mixed

    def load(head, part):
        span = slice(part * half, (part + 1) * half)
        at = head % 2
        return top_buf[at, span, 0:1], sum_buf[at, span, 0:1], mix_buf[at, span, :]

    def store(head, part, state):
        span = slice(part * half, (part + 1) * half)
        at = head % 2
        top_buf[at, span, 0:1] = state[0]
        sum_buf[at, span, 0:1] = state[1]
        mix_buf[at, span, :] = state[2]

    def turn(at, carry):
        @pl.when(at < AH)
        def _():
            head = at
            gone(0, head, me + 4 < n)
            gone(1, head, upper == 0)

            @pl.when(head + AHEAD < AH)
            def _():
                send_own(head + AHEAD)

            for w in (0, 1):
                for piece in range(PIECES[0]):
                    arrived(0, head, me >= 4, (w,), (piece,))
                    begin((upper == 1) & (me >= 4), 1, head, 0, beside, (w,), (piece,))
                begin((odd == 1) & (me >= 4), 3, head, 0, twin, (w,))

        @pl.when(at >= 1)
        def _():
            head = at - 1
            for w in (0, 1):
                arrived(1, head, me >= 2, (w,))
                begin((odd == 1) & (me >= 2), 2, head, 2, twin, (w,))
                begin((odd == 0) & (me >= 2), 3, head, 2, twin, (w,))

        @pl.when(at < AH)
        def _():
            head = at
            for copy in own_copies(head):
                copy.wait()
            for part in (0, 1):
                store(head, part, absorb(None, part, head, (
                    (part * half, rows - part * half), (WINDOW, (part + 1) * half)
                )))

        @pl.when(at >= 1)
        def _():
            head = at - 1
            for part in (0, 1):
                store(head, part, absorb(load(head, part), part, head, ((2 * rows, rows),)))
            arrived(2, head, me >= 1)
            arrived(3, head, me >= 3)
            for part in (0, 1):
                span = slice(part * half, (part + 1) * half)
                _, total, mixed = absorb(load(head, part), part, head, ((rows, rows), (3 * rows, rows)))
                out_ref[span, pl.ds(pl.multiple_of(head * DH, DH), DH)] = (mixed / total).astype(jnp.bfloat16)

        return carry

    lax.fori_loop(0, AH + 1, turn, 0)

    def finish(head, carry):
        gone(1, head, (upper == 1) & (me >= 4))
        gone(2, head, (odd == 0) | (me >= 2))
        gone(3, head, ((odd == 0) & (me >= 2)) | (me >= 5))
        return carry

    lax.fori_loop(0, AH, finish, 0)


def local(query_rows, key_rows, value_rows, doc_start, n):
    rows = query_rows.shape[0]
    reach = WINDOW // rows + 1
    anywhere = pl.BlockSpec(memory_space=pltpu.HBM)
    inside = pl.BlockSpec(memory_space=pltpu.VMEM)
    return pl.pallas_call(
        functools.partial(kernel, n, rows),
        out_shape=pltpu.VMEM(query_rows.shape, jnp.bfloat16),
        in_specs=[anywhere, anywhere, anywhere, anywhere],
        out_specs=inside,
        scratch_shapes=[
            pltpu.VMEM((AH, rows, DH), jnp.bfloat16),
            pltpu.VMEM((AH, reach * rows, DH), jnp.bfloat16),
            pltpu.VMEM((AH, reach * rows, DH), jnp.bfloat16),
            pltpu.VMEM((1, rows), jnp.int32),
            pltpu.VMEM((rows, DH), jnp.int32),
            pltpu.VMEM((2, rows, DH), jnp.float32),
            pltpu.VMEM((2, rows, DH), jnp.float32),
            pltpu.VMEM((2, rows, DH), jnp.float32),
            pltpu.SemaphoreType.DMA((3, AH)),
            pltpu.SemaphoreType.DMA,
            pltpu.SemaphoreType.DMA((4, 2, max(PIECES), AH)),
            pltpu.SemaphoreType.DMA((4, 2, max(PIECES), AH)),
        ],
        compiler_params=pltpu.CompilerParams(
            collective_id=0, has_side_effects=True, vmem_limit_bytes=48 * 1024 * 1024
        ),
    )(*(pltpu.with_memory_space_constraint(x, pltpu.HBM)
        for x in (doc_start.reshape(1, rows), query_rows, key_rows, value_rows)))


def solution(mesh):
    placed = (
        P(("grp", "seq"), None),
        P(("grp", "seq"), None),
        P(("grp", "seq"), None),
        P(("grp", "seq")),
    )
    return jax.shard_map(
        functools.partial(local, n=mesh.shape["seq"]),
        mesh=mesh, in_specs=placed, out_specs=P(("grp", "seq"), None), check_vma=False,
    )
```

```python
import functools
import math

import jax
import jax.numpy as jnp
from jax import lax
from jax.experimental import pallas as pl
from jax.experimental.pallas import tpu as pltpu
from jax.sharding import PartitionSpec as P

AH = 12
DH = 128
WINDOW = 2048
MESH = pl.DeviceIdType.MESH
HIDDEN = -1e30
KEYS_AHEAD = 3
KEYS_TURN = 2
BESIDE_AHEAD = 1
QUERIES_AHEAD = 3
OUTER, BESIDE = 0, 1
NEXT, ACROSS, NEAR, FAR, AFTER = 0, 1, 2, 3, 4
LANDING = (0, 2, 3, 1, 5)


def kernel(n, rows, doc_hbm, q_hbm, k_hbm, v_hbm, out_ref,
           q_buf, asked, k_buf, v_buf, doc_buf, low, top_buf, sum_buf, mix_buf,
           own_mix, own_log, held_mix, held_log, sent_mix, sent_log, got_mix, got_log,
           own_sem, doc_sem, doc_send, doc_recv, send_sem, recv_sem, q_send, q_recv, o_send, o_recv):
    group = lax.axis_index("grp")
    me = lax.axis_index("seq")
    planes = n // 4
    plane = me // 4
    upper = (me // 2) % 2
    odd = me % 2
    beside = me + 2 - 4 * upper
    twin = me + 1 - 2 * odd
    half = rows // 2
    sources = (k_hbm, v_hbm)
    buffers = (k_buf, v_buf)
    first = plane == 0
    last = plane == planes - 1

    moved = AH * (planes - plane) // planes
    moved_next = AH * (planes - 1 - plane) // planes
    asked_beside = upper * moved_next + (1 - upper) * moved
    asks_beside = upper * moved + (1 - upper) * moved_next

    def columns(ref, head):
        return ref.at[pl.ds(0, rows), pl.ds(pl.multiple_of(head * DH, DH), DH)]

    def slot(which, head, shard):
        return buffers[which].at[head, pl.ds(shard * rows, rows), :]

    def own_copies(head):
        pairs = [(q_hbm, q_buf.at[head])] + [(sources[w], slot(w, head, 4)) for w in (0, 1)]
        return [
            pltpu.make_async_copy(columns(source, head), target, own_sem.at[at, head])
            for at, (source, target) in enumerate(pairs)
        ]

    def remote(source, target, send, recv, device):
        return pltpu.make_async_remote_copy(
            src_ref=source, dst_ref=target, send_sem=send, recv_sem=recv,
            device_id=(group, device), device_id_type=MESH,
        )

    def kv_copy(kind, head, w, source_shard, device):
        source = columns(sources[w], head) if source_shard is None else slot(w, head, source_shard)
        return remote(source, slot(w, head, LANDING[kind]), send_sem.at[kind, w, head], recv_sem.at[kind, w, head], device)

    def begin(condition, kind, head, source_shard, device, which=(0, 1)):
        @pl.when(condition)
        def _():
            for w in which:
                kv_copy(kind, head, w, source_shard, device).start()

    def arrived(kind, head, condition, which=(0, 1)):
        @pl.when(condition)
        def _():
            for w in which:
                kv_copy(kind, head, w, None, twin).wait_recv()

    def gone(kind, head, condition):
        @pl.when(condition)
        def _():
            for w in (0, 1):
                kv_copy(kind, head, w, None, twin).wait_send()

    def q_copy(way, head, source, device):
        source = columns(q_hbm, head) if source is None else source
        return remote(source, asked.at[way, head], q_send.at[way, head], q_recv.at[way, head], device)

    def doc_copy(way, source, device):
        return remote(source, doc_buf.at[1 + way], doc_send.at[way], doc_recv.at[way], device)

    def back_copies(way, head, device):
        return [
            remote(sent_mix.at[way, head], got_mix.at[way, head], o_send.at[way, 0, head], o_recv.at[way, 0, head], device),
            remote(sent_log.at[way, head], got_log.at[way, head], o_send.at[way, 1, head], o_recv.at[way, 1, head], device),
        ]

    doc_own = pltpu.make_async_copy(doc_hbm, doc_buf.at[0], doc_sem)
    doc_own.start()
    barrier = pltpu.get_barrier_semaphore()
    pl.semaphore_signal(barrier, inc=1, device_id=(group, beside), device_id_type=MESH)
    pl.semaphore_signal(barrier, inc=1, device_id=(group, twin), device_id_type=MESH)

    @pl.when(me >= 4)
    def _():
        pl.semaphore_signal(barrier, inc=1, device_id=(group, me - 4), device_id_type=MESH)

    @pl.when(me + 4 < n)
    def _():
        pl.semaphore_signal(barrier, inc=1, device_id=(group, me + 4), device_id_type=MESH)

    peers = 2 + (me >= 4).astype(jnp.int32) + (me + 4 < n).astype(jnp.int32)
    pl.semaphore_wait(barrier, peers)

    def send_next(at):
        head = moved_next + at
        begin((me + 4 < n) & (head < AH), NEXT, head, None, me + 4)

    def send_beside(at):
        head = moved + at
        begin((upper == 0) & (head < AH), ACROSS, head, None, beside)

    def send_query(head):
        @pl.when((upper == 1) & (head < moved))
        def _():
            q_copy(BESIDE, head, None, beside).start()

    @pl.when(me >= 4)
    def _():
        doc_copy(OUTER, doc_hbm, me - 4).start()

    @pl.when(upper == 1)
    def _():
        doc_copy(BESIDE, doc_hbm, beside).start()

    for at in range(max(KEYS_AHEAD, BESIDE_AHEAD, QUERIES_AHEAD)):
        @pl.when((me >= 4) & (at < moved))
        def _():
            q_copy(OUTER, at, None, me - 4).start()

        if at < QUERIES_AHEAD:
            send_query(at)
        if at < BESIDE_AHEAD:
            send_beside(at)
        if at < KEYS_AHEAD:
            send_next(at)

    def opening(head, carry):
        @pl.when((me >= 4) & (head < moved) & (head >= max(KEYS_AHEAD, BESIDE_AHEAD, QUERIES_AHEAD)))
        def _():
            q_copy(OUTER, head, None, me - 4).start()

        for copy in own_copies(head):
            copy.start()
        begin(odd == 0, NEAR, head, None, twin)
        begin((odd == 1) & (head < asked_beside), AFTER, head, None, twin)
        return carry

    lax.fori_loop(0, AH, opening, 0)

    row = lax.broadcasted_iota(jnp.int32, (rows, DH), 0)

    def column(values, count):
        return jnp.transpose(jnp.broadcast_to(values, (DH, count)))

    def set_low(at, distance):
        starts = column(doc_buf[at], rows)
        low[at] = jnp.maximum(starts - (me * rows - WINDOW), row + (1 + distance * rows))

    doc_own.wait()
    set_low(0, 0)

    def own_wait(head, carry):
        for copy in own_copies(head):
            copy.wait()
        return carry

    lax.fori_loop(0, AH, own_wait, 0)

    scale = math.log2(math.e) / math.sqrt(DH)

    def absorb(state, part, head, spans, source=None):
        span = slice(part * half, (part + 1) * half)
        queries = q_buf[head, span, :] if source is None else asked[source, head, span, :]
        lowest = low[0 if source is None else 1 + source, span, 0:1]
        every = []
        for start, count, upto in spans:
            scores = lax.dot_general(
                queries, k_buf[head, pl.ds(start, count), :], (((1,), (1,)), ((), ())),
                preferred_element_type=jnp.float32,
            )
            place = start + lax.broadcasted_iota(jnp.int32, (half, count), 1)
            allowed = place >= lowest
            if upto:
                query = part * half + lax.broadcasted_iota(jnp.int32, (half, count), 0)
                allowed = allowed & (place <= query + WINDOW)
            every.append(jnp.where(allowed, scores, HIDDEN))
        largest = functools.reduce(jnp.maximum, [jnp.max(x, axis=1, keepdims=True) for x in every])
        if state is not None:
            largest = jnp.maximum(largest, state[0])
        total = mixed = 0.0
        if state is not None:
            fade = jnp.exp2((state[0] - largest) * scale)
            total, mixed = state[1] * fade, state[2] * fade
        for (start, count, _), scores in zip(spans, every):
            powers = jnp.exp2((scores - largest) * scale)
            total = total + jnp.sum(powers, axis=1, keepdims=True)
            mixed = mixed + jnp.dot(
                powers.astype(jnp.bfloat16), v_buf[head, pl.ds(start, count), :],
                preferred_element_type=jnp.float32,
            )
        return largest, total, mixed

    def load(head, part):
        span = slice(part * half, (part + 1) * half)
        at = head % 2
        return top_buf[at, span, 0:1], sum_buf[at, span, 0:1], mix_buf[at, span, :]

    def store(head, part, state):
        span = slice(part * half, (part + 1) * half)
        at = head % 2
        top_buf[at, span, 0:1] = state[0]
        sum_buf[at, span, 0:1] = state[1]
        mix_buf[at, span, :] = state[2]

    def emit(head, part, values):
        span = slice(part * half, (part + 1) * half)
        out_ref[span, pl.ds(pl.multiple_of(head * DH, DH), DH)] = values.astype(jnp.bfloat16)

    def closed(state):
        largest, total, mixed = state
        return mixed / total, largest * scale + jnp.log2(total)

    def put_back(way, head, part, mixed, log):
        span = slice(part * half, (part + 1) * half)
        sent_mix[way, head, span, :] = mixed.astype(jnp.bfloat16)
        sent_log[way, head, :, span] = jnp.transpose(jnp.broadcast_to(log, (half, DH)))[0:1, :]

    def take_back(way, head, part):
        span = slice(part * half, (part + 1) * half)
        return got_mix[way, head, span, :].astype(jnp.float32), column(got_log[way, head, :, span], half)[:, 0:1]

    def merged(pieces):
        largest = functools.reduce(jnp.maximum, [log for _, log in pieces])
        total = mixed = 0.0
        for values, log in pieces:
            weight = jnp.exp2(log - largest)
            total = total + weight
            mixed = mixed + values * weight
        return mixed / total, largest + jnp.log2(total)

    def beside_service(head):
        q_copy(BESIDE, head, None, twin).wait_recv()
        start = pl.multiple_of((4 - odd) * rows, rows)
        for part in (0, 1):
            put_back(BESIDE, head, part, *closed(absorb(None, part, head, ((start, 2 * rows, False),), BESIDE)))
        for copy in back_copies(BESIDE, head, beside):
            copy.start()

    def outer_service(head, count):
        for part in (0, 1):
            span = slice(part * half, (part + 1) * half)
            mixed, log = closed(absorb(
                None, part, head, ((WINDOW + part * half, count - part * half, False),), OUTER))

            @pl.when(upper == 1)
            def _():
                put_back(OUTER, head, part, mixed, log)

            @pl.when(upper == 0)
            def _():
                held_mix[head % 4, span, :] = mixed
                held_log[head % 4, span, 0:1] = log

    def own_part(head, start):
        for part in (0, 1):
            span = slice(part * half, (part + 1) * half)
            mixed, log = closed(absorb(None, part, head, ((start, WINDOW + (part + 1) * half - start, True),)))
            own_mix[head, span, :] = mixed
            own_log[head, span, 0:1] = log

    final_lag = jnp.where(first, 1, jnp.maximum(3, AH - moved))

    def turn(at, carry):
        for extra in range(KEYS_TURN):
            send_next(KEYS_AHEAD + at * KEYS_TURN + extra)
        send_beside(at + BESIDE_AHEAD)
        send_query(at + QUERIES_AHEAD)

        arrived(NEAR, at, (odd == 1) & (at < moved))
        arrived(AFTER, at, (odd == 0) & (at < asked_beside))

        @pl.when((at == 0) & jnp.logical_not(last))
        def _():
            doc_copy(OUTER, doc_hbm, twin).wait_recv()
            set_low(1 + OUTER, 4)

            @pl.when(upper == 0)
            def _():
                doc_copy(BESIDE, doc_buf.at[1 + OUTER], beside).start()

        @pl.when(at < moved_next)
        def _():
            q_copy(OUTER, at, None, twin).wait_recv()

            @pl.when(upper == 0)
            def _():
                q_copy(BESIDE, at, asked.at[OUTER, at], beside).start()

        served = at - upper

        @pl.when((served == 0) & (served < asked_beside))
        def _():
            doc_copy(BESIDE, doc_hbm, twin).wait_recv()
            set_low(1 + BESIDE, 2)

        @pl.when((served >= 0) & (served < asked_beside))
        def _():
            beside_service(served)

        @pl.when((at < moved_next) & (odd == 0))
        def _():
            outer_service(at, 2 * rows)

        @pl.when((at < moved_next) & (odd == 1))
        def _():
            outer_service(at, rows)

        @pl.when((at < moved_next) & (upper == 1))
        def _():
            for copy in back_copies(OUTER, at, me + 4):
                copy.start()

        joined = at - 2

        @pl.when((upper == 0) & (joined >= 0) & (joined < moved_next))
        def _():
            for copy in back_copies(BESIDE, joined, twin):
                copy.wait_recv()
            for part in (0, 1):
                span = slice(part * half, (part + 1) * half)
                here = held_mix[joined % 4, span, :], held_log[joined % 4, span, 0:1]
                put_back(OUTER, joined, part, *merged([here, take_back(BESIDE, joined, part)]))
            for copy in back_copies(OUTER, joined, me + 4):
                copy.start()

        @pl.when((at < moved) & (odd == 0))
        def _():
            own_part(at, WINDOW)

        @pl.when((at < moved) & (odd == 1))
        def _():
            own_part(at, WINDOW - rows)

        entering = moved + at
        leaving = entering - 1

        @pl.when(entering < AH)
        def _():
            for w in (0, 1):
                arrived(NEXT, entering, True, (w,))
                begin(upper == 1, ACROSS, entering, 0, beside, (w,))
                begin(odd == 1, FAR, entering, 0, twin, (w,))

        @pl.when((at >= 1) & (leaving < AH))
        def _():
            for w in (0, 1):
                arrived(ACROSS, leaving, True, (w,))
                begin(odd == 1, NEAR, leaving, 2, twin, (w,))
                begin(odd == 0, FAR, leaving, 2, twin, (w,))

        @pl.when(entering < AH)
        def _():
            for part in (0, 1):
                store(entering, part, absorb(None, part, entering, (
                    (part * half, rows - part * half, False), (WINDOW, (part + 1) * half, True)
                )))

        @pl.when((at >= 1) & (leaving < AH))
        def _():
            for part in (0, 1):
                store(leaving, part, absorb(load(leaving, part), part, leaving, ((2 * rows, rows, False),)))
            arrived(NEAR, leaving, True)
            arrived(FAR, leaving, True)
            for part in (0, 1):
                _, total, mixed = absorb(load(leaving, part), part, leaving, ((rows, rows, False), (3 * rows, rows, False)))
                emit(leaving, part, mixed / total)

        done = at - final_lag

        @pl.when((done >= 0) & (done < moved))
        def _():
            @pl.when(upper == 1)
            def _():
                for copy in back_copies(BESIDE, done, twin):
                    copy.wait_recv()

            @pl.when(plane >= 1)
            def _():
                for copy in back_copies(OUTER, done, twin):
                    copy.wait_recv()

            for part in (0, 1):
                span = slice(part * half, (part + 1) * half)
                here = own_mix[done, span, :], own_log[done, span, 0:1]

                @pl.when(first & (upper == 0))
                def _():
                    emit(done, part, here[0])

                @pl.when(first & (upper == 1))
                def _():
                    emit(done, part, merged([here, take_back(BESIDE, done, part)])[0])

                @pl.when((plane >= 1) & (upper == 0))
                def _():
                    emit(done, part, merged([here, take_back(OUTER, done, part)])[0])

                @pl.when((plane >= 1) & (upper == 1))
                def _():
                    emit(done, part, merged([here, take_back(OUTER, done, part), take_back(BESIDE, done, part)])[0])

        return carry

    lax.fori_loop(0, AH + 3, turn, 0)

    def finish(head, carry):
        gone(NEXT, head, (me + 4 < n) & (head >= moved_next))
        gone(ACROSS, head, head >= moved)
        gone(NEAR, head, (odd == 0) | (head >= moved))
        gone(FAR, head, head >= moved)
        gone(AFTER, head, (odd == 1) & (head < asked_beside))

        @pl.when((plane >= 1) & (head < moved))
        def _():
            q_copy(OUTER, head, None, twin).wait_send()

        @pl.when(head < asks_beside)
        def _():
            q_copy(BESIDE, head, None, twin).wait_send()

        @pl.when(head < asked_beside)
        def _():
            for copy in back_copies(BESIDE, head, twin):
                copy.wait_send()

        @pl.when(head < moved_next)
        def _():
            for copy in back_copies(OUTER, head, twin):
                copy.wait_send()

        return carry

    lax.fori_loop(0, AH, finish, 0)

    @pl.when(me >= 4)
    def _():
        doc_copy(OUTER, doc_hbm, twin).wait_send()

    @pl.when((upper == 1) | jnp.logical_not(last))
    def _():
        doc_copy(BESIDE, doc_hbm, twin).wait_send()


def local(query_rows, key_rows, value_rows, doc_start, n):
    rows = query_rows.shape[0]
    reach = WINDOW // rows + 2
    operands = [
        pltpu.with_memory_space_constraint(x, pltpu.HBM)
        for x in (doc_start.reshape(1, rows), query_rows, key_rows, value_rows)
    ]
    mix, log = (2, AH, rows, DH), (2, AH, 1, rows)
    return pl.pallas_call(
        functools.partial(kernel, n, rows),
        out_shape=pltpu.VMEM(query_rows.shape, jnp.bfloat16),
        in_specs=[pl.BlockSpec(memory_space=pltpu.HBM)] * 4,
        out_specs=pl.BlockSpec(memory_space=pltpu.VMEM),
        scratch_shapes=[
            pltpu.VMEM((AH, rows, DH), jnp.bfloat16),
            pltpu.VMEM(mix, jnp.bfloat16),
            pltpu.VMEM((AH, reach * rows, DH), jnp.bfloat16),
            pltpu.VMEM((AH, reach * rows, DH), jnp.bfloat16),
            pltpu.VMEM((3, 1, rows), jnp.int32),
            pltpu.VMEM((3, rows, DH), jnp.int32),
            pltpu.VMEM((2, rows, DH), jnp.float32),
            pltpu.VMEM((2, rows, DH), jnp.float32),
            pltpu.VMEM((2, rows, DH), jnp.float32),
            pltpu.VMEM((AH, rows, DH), jnp.float32),
            pltpu.VMEM((AH, rows, DH), jnp.float32),
            pltpu.VMEM((4, rows, DH), jnp.float32),
            pltpu.VMEM((4, rows, DH), jnp.float32),
            pltpu.VMEM(mix, jnp.bfloat16),
            pltpu.VMEM(log, jnp.float32),
            pltpu.VMEM(mix, jnp.bfloat16),
            pltpu.VMEM(log, jnp.float32),
            pltpu.SemaphoreType.DMA((3, AH)),
            pltpu.SemaphoreType.DMA,
            pltpu.SemaphoreType.DMA((2,)),
            pltpu.SemaphoreType.DMA((2,)),
            pltpu.SemaphoreType.DMA((5, 2, AH)),
            pltpu.SemaphoreType.DMA((5, 2, AH)),
            pltpu.SemaphoreType.DMA((2, AH)),
            pltpu.SemaphoreType.DMA((2, AH)),
            pltpu.SemaphoreType.DMA((2, 2, AH)),
            pltpu.SemaphoreType.DMA((2, 2, AH)),
        ],
        compiler_params=pltpu.CompilerParams(
            collective_id=0, has_side_effects=True, vmem_limit_bytes=56 * 1024 * 1024
        ),
    )(*operands)


def solution(mesh):
    placed = (
        P(("grp", "seq"), None),
        P(("grp", "seq"), None),
        P(("grp", "seq"), None),
        P(("grp", "seq")),
    )
    return jax.shard_map(
        functools.partial(local, n=mesh.shape["seq"]),
        mesh=mesh, in_specs=placed, out_specs=P(("grp", "seq"), None), check_vma=False,
    )
```

```python
import functools
import math

import jax
import jax.numpy as jnp
from jax import lax
from jax.experimental import pallas as pl
from jax.experimental.pallas import tpu as pltpu
from jax.sharding import PartitionSpec as P

AH = 12
DH = 128
WINDOW = 2048
MESH = pl.DeviceIdType.MESH
HIDDEN = -1e30
KEYS_AHEAD = 6
JOIN_LAG = 3
FINAL_LAG = 2
KEYS_TURN = 2
BESIDE_AHEAD = 1
QUERIES_AHEAD = 3
OUTER, BESIDE = 0, 1
NEXT, ACROSS, NEAR, FAR, AFTER = 0, 1, 2, 3, 4
CUTS = 2
WIDE = 2
LANDING = (0, 2, 3, 1, 5)
FROM_BESIDE, FROM_BESIDE_TOO, FROM_BEHIND, FROM_AHEAD, FROM_TWIN, FROM_HERE = 0, 1, 2, 3, 4, 5
TO_AHEAD, TO_BEHIND, TO_BESIDE, TO_BESIDE_TOO, TO_TWIN = 0, 1, 2, 3, 4
KV_RECV = (FROM_BEHIND, FROM_BESIDE, FROM_TWIN, FROM_BESIDE_TOO, FROM_TWIN)
KV_SEND = (TO_AHEAD, TO_BESIDE, TO_TWIN, TO_BEHIND, TO_TWIN)


def kernel(n, rows, doc_hbm, q_hbm, k_hbm, v_hbm, out_ref,
           q_buf, asked, k_buf, v_buf, doc_buf, low, top_buf, sum_buf, mix_buf,
           own_mix, own_log, held_mix, held_log, sent_mix, sent_log, got_mix, got_log,
           doc_sem, doc_send, doc_recv, send_sem, recv_sem):
    group = lax.axis_index("grp")
    me = lax.axis_index("seq")
    planes = n // 4
    plane = me // 4
    upper = (me // 2) % 2
    odd = me % 2
    beside = me + 2 - 4 * upper
    twin = me + 1 - 2 * odd
    halves = [(at * (rows // CUTS), rows // CUTS) for at in range(CUTS)]
    wholes = [(at * (rows // WIDE), rows // WIDE) for at in range(WIDE)]
    sources = (k_hbm, v_hbm)
    buffers = (k_buf, v_buf)
    first = plane == 0
    last = plane == planes - 1

    moved = AH * (planes - plane) // planes
    moved_next = AH * (planes - 1 - plane) // planes
    asked_beside = upper * moved_next + (1 - upper) * moved

    def columns(ref, head):
        return ref.at[pl.ds(0, rows), pl.ds(pl.multiple_of(head * DH, DH), DH)]

    def slot(which, head, shard):
        return buffers[which].at[head, pl.ds(shard * rows, rows), :]

    def own_copies(head):
        pairs = [(q_hbm, q_buf.at[head])] + [(sources[w], slot(w, head, 4)) for w in (0, 1)]
        return [
            pltpu.make_async_copy(columns(source, head), target, recv_sem.at[FROM_HERE, head])
            for source, target in pairs
        ]

    def remote(source, target, send, recv, device):
        return pltpu.make_async_remote_copy(
            src_ref=source, dst_ref=target, send_sem=send, recv_sem=recv,
            device_id=(group, device), device_id_type=MESH,
        )

    block, pair, three, answer = rows, 2 * rows, 3 * rows, rows + 16

    def settle(sem, size):
        view = k_buf.at[0, pl.ds(0, size), :]
        pltpu.make_async_copy(view, view, sem).wait()

    def received(at, head, size):
        settle(recv_sem.at[at, head], size)

    def sent(condition, at, head, size):
        @pl.when(condition)
        def _():
            settle(send_sem.at[at, head], size)

    def begin(condition, kind, head, source_shard, device):
        @pl.when(condition)
        def _():
            for w in (0, 1):
                source = columns(sources[w], head) if source_shard is None else slot(w, head, source_shard)
                remote(source, slot(w, head, LANDING[kind]), send_sem.at[KV_SEND[kind], head],
                       recv_sem.at[KV_RECV[kind], head], device).start()

    def arrived(kind, head, condition):
        @pl.when(condition)
        def _():
            received(KV_RECV[kind], head, pair)

    def ask_behind(head):
        remote(columns(q_hbm, head), asked.at[OUTER, head], send_sem.at[TO_BEHIND, head],
               recv_sem.at[FROM_AHEAD, head], me - 4).start()

    def ask_beside(head, source, send, recv):
        remote(source, asked.at[BESIDE, head], send_sem.at[send, head], recv_sem.at[recv, head], beside).start()

    def doc_copy(way, source, device):
        return remote(source, doc_buf.at[1 + way], doc_send.at[way], doc_recv.at[way], device)

    def give_back(way, head, send, recv, device):
        for source, target in ((sent_mix, got_mix), (sent_log, got_log)):
            remote(source.at[way, head], target.at[way, head], send_sem.at[send, head],
                   recv_sem.at[recv, head], device).start()

    doc_own = pltpu.make_async_copy(doc_hbm, doc_buf.at[0], doc_sem)
    doc_own.start()
    barrier = pltpu.get_barrier_semaphore()
    pl.semaphore_signal(barrier, inc=1, device_id=(group, beside), device_id_type=MESH)
    pl.semaphore_signal(barrier, inc=1, device_id=(group, twin), device_id_type=MESH)

    @pl.when(me >= 4)
    def _():
        pl.semaphore_signal(barrier, inc=1, device_id=(group, me - 4), device_id_type=MESH)

    @pl.when(me + 4 < n)
    def _():
        pl.semaphore_signal(barrier, inc=1, device_id=(group, me + 4), device_id_type=MESH)

    def fetch(head, carry):
        for copy in own_copies(head):
            copy.start()
        return carry

    lax.fori_loop(0, AH, fetch, 0)

    peers = 2 + (me >= 4).astype(jnp.int32) + (me + 4 < n).astype(jnp.int32)
    pl.semaphore_wait(barrier, peers)

    def send_next(at):
        head = moved_next + at
        begin((me + 4 < n) & (head < AH), NEXT, head, None, me + 4)

    def send_beside(at):
        head = moved + at
        begin((upper == 0) & (head < AH), ACROSS, head, None, beside)

    def send_query(head):
        @pl.when((upper == 1) & (head < moved))
        def _():
            ask_beside(head, columns(q_hbm, head), TO_BESIDE, FROM_BESIDE)

    @pl.when(me >= 4)
    def _():
        doc_copy(OUTER, doc_hbm, me - 4).start()

    @pl.when(upper == 1)
    def _():
        doc_copy(BESIDE, doc_hbm, beside).start()

    for at in range(max(KEYS_AHEAD, BESIDE_AHEAD, QUERIES_AHEAD)):
        @pl.when((me >= 4) & (at < moved))
        def _():
            ask_behind(at)

        if at < QUERIES_AHEAD:
            send_query(at)
        if at < BESIDE_AHEAD:
            send_beside(at)
        if at < KEYS_AHEAD:
            send_next(at)

    def opening(head, carry):
        @pl.when((me >= 4) & (head < moved) & (head >= max(KEYS_AHEAD, BESIDE_AHEAD, QUERIES_AHEAD)))
        def _():
            ask_behind(head)

        begin(odd == 0, NEAR, head, None, twin)
        begin((odd == 1) & (head < asked_beside), AFTER, head, None, twin)
        return carry

    lax.fori_loop(0, AH, opening, 0)

    row = lax.broadcasted_iota(jnp.int32, (rows, DH), 0)

    def column(values, count):
        return jnp.transpose(jnp.broadcast_to(values, (DH, count)))

    def set_low(at, distance):
        starts = column(doc_buf[at], rows)
        low[at] = jnp.maximum(starts - (me * rows - WINDOW), row + (1 + distance * rows))

    doc_own.wait()
    set_low(0, 0)

    def own_wait(head, condition):
        @pl.when(condition)
        def _():
            received(FROM_HERE, head, three)

    scale = math.log2(math.e) / math.sqrt(DH)

    def across(values, count):
        return values if count == DH else jnp.concatenate([values] * (count // DH), axis=1)

    def absorb(jobs, head, source=None):
        scored = []
        for state, part, spans in jobs:
            span = slice(part[0], part[0] + part[1])
            queries = q_buf[head, span, :] if source is None else asked[source, head, span, :]
            lowest = low[0 if source is None else 1 + source, span, :]
            every = []
            for start, count, upto in spans:
                scores = lax.dot_general(
                    queries, k_buf[head, pl.ds(start, count), :], (((1,), (1,)), ((), ())),
                    preferred_element_type=jnp.float32,
                )
                place = start + lax.broadcasted_iota(jnp.int32, (part[1], count), 1)
                allowed = place >= across(lowest, count)
                if upto:
                    query = part[0] + lax.broadcasted_iota(jnp.int32, (part[1], count), 0)
                    allowed = allowed & (place <= query + WINDOW)
                every.append(jnp.where(allowed, scores, HIDDEN))
            scored.append(every)
        results = []
        for (state, part, spans), every in zip(jobs, scored):
            largest = functools.reduce(jnp.maximum, [jnp.max(x, axis=1, keepdims=True) for x in every])
            largest = jnp.broadcast_to(largest, (part[1], DH))
            if state is not None:
                largest = jnp.maximum(largest, state[0])
            total = mixed = 0.0
            if state is not None:
                fade = jnp.exp2((state[0] - largest) * scale)
                total, mixed = state[1] * fade, state[2] * fade
            for (start, count, _), scores in zip(spans, every):
                powers = jnp.exp2((scores - across(largest, count)) * scale)
                total = total + jnp.broadcast_to(jnp.sum(powers, axis=1, keepdims=True), (part[1], DH))
                mixed = mixed + jnp.dot(
                    powers.astype(jnp.bfloat16), v_buf[head, pl.ds(start, count), :],
                    preferred_element_type=jnp.float32,
                )
            results.append((largest, total, mixed))
        return results

    def load(head, part):
        span = slice(part[0], part[0] + part[1])
        at = head % 2
        return top_buf[at, span, :], sum_buf[at, span, :], mix_buf[at, span, :]

    def store(head, part, state):
        span = slice(part[0], part[0] + part[1])
        at = head % 2
        top_buf[at, span, :] = state[0]
        sum_buf[at, span, :] = state[1]
        mix_buf[at, span, :] = state[2]

    def emit(head, part, values):
        span = slice(part[0], part[0] + part[1])
        out_ref[span, pl.ds(pl.multiple_of(head * DH, DH), DH)] = values.astype(jnp.bfloat16)

    def closed(state):
        largest, total, mixed = state
        return mixed / total, largest * scale + jnp.log2(total)

    def put_back(way, head, part, mixed, log):
        span = slice(part[0], part[0] + part[1])
        sent_mix[way, head, span, :] = mixed.astype(jnp.bfloat16)
        sent_log[way, head, :, span] = jnp.transpose(log)[0:2, :]

    def take_back(way, head, part):
        span = slice(part[0], part[0] + part[1])
        return got_mix[way, head, span, :].astype(jnp.float32), column(got_log[way, head, 0:1, span], part[1])

    def merged(pieces):
        largest = functools.reduce(jnp.maximum, [log for _, log in pieces])
        total = mixed = 0.0
        for values, log in pieces:
            weight = jnp.exp2(log - largest)
            total = total + weight
            mixed = mixed + values * weight
        return mixed / total, largest + jnp.log2(total)

    def beside_service(head):
        received(upper, head, block)
        start = pl.multiple_of((4 - odd) * rows, rows)
        states = absorb([(None, part, ((start, 2 * rows, False),)) for part in wholes], head, BESIDE)
        for part, state in zip(wholes, states):
            put_back(BESIDE, head, part, *closed(state))
        give_back(BESIDE, head, TO_BESIDE + upper, upper, beside)

    def outer_service(head, count):
        states = absorb([(None, part, ((WINDOW + part[0], count - part[0], False),)) for part in halves], head, OUTER)
        for part, state in zip(halves, states):
            span = slice(part[0], part[0] + part[1])
            mixed, log = closed(state)

            @pl.when(upper == 1)
            def _():
                put_back(OUTER, head, part, mixed, log)

            @pl.when(upper == 0)
            def _():
                held_mix[head % 4, span, :] = mixed
                held_log[head % 4, span, :] = log

    def own_part(head, start):
        states = absorb([(None, part, ((start, WINDOW + part[0] + part[1] - start, True),)) for part in halves], head)
        for part, state in zip(halves, states):
            span = slice(part[0], part[0] + part[1])
            mixed, log = closed(state)
            own_mix[head, span, :] = mixed
            own_log[head, span, :] = log

    final_lag = jnp.maximum(FINAL_LAG, AH - moved)

    def turn(at, carry):
        entering = moved + at
        leaving = entering - 1

        own_wait(at, at < moved)
        own_wait(moved + at, moved + at < AH)
        arrived(NEAR, at, (odd == 1) & (at < moved))
        arrived(AFTER, at, (odd == 0) & (at < asked_beside))

        @pl.when(entering < AH)
        def _():
            arrived(NEXT, entering, True)
            begin(upper == 1, ACROSS, entering, 0, beside)
            begin(odd == 1, FAR, entering, 0, twin)

        @pl.when((at == 0) & jnp.logical_not(last))
        def _():
            doc_copy(OUTER, doc_hbm, twin).wait_recv()
            set_low(1 + OUTER, 4)

            @pl.when(upper == 0)
            def _():
                doc_copy(BESIDE, doc_buf.at[1 + OUTER], beside).start()

        @pl.when(at < moved_next)
        def _():
            received(FROM_AHEAD, at, block)

            @pl.when(upper == 0)
            def _():
                ask_beside(at, asked.at[OUTER, at], TO_BESIDE_TOO, FROM_BESIDE_TOO)

        @pl.when((at < moved) & (odd == 0))
        def _():
            own_part(at, WINDOW)

        @pl.when((at < moved) & (odd == 1))
        def _():
            own_part(at, WINDOW - rows)

        @pl.when((at >= 1) & (leaving < AH))
        def _():
            arrived(ACROSS, leaving, True)
            begin(odd == 1, NEAR, leaving, 2, twin)
            begin(odd == 0, FAR, leaving, 2, twin)

        for extra in range(KEYS_TURN):
            send_next(KEYS_AHEAD + at * KEYS_TURN + extra)
        send_beside(at + BESIDE_AHEAD)
        send_query(at + QUERIES_AHEAD)

        served = at - upper

        @pl.when((served == 0) & (served < asked_beside))
        def _():
            doc_copy(BESIDE, doc_hbm, twin).wait_recv()
            set_low(1 + BESIDE, 2)

        @pl.when((served >= 0) & (served < asked_beside))
        def _():
            beside_service(served)

        @pl.when((at < moved_next) & (odd == 0))
        def _():
            outer_service(at, 2 * rows)

        @pl.when((at < moved_next) & (odd == 1))
        def _():
            outer_service(at, rows)

        @pl.when((at < moved_next) & (upper == 1))
        def _():
            give_back(OUTER, at, TO_AHEAD, FROM_BEHIND, me + 4)

        @pl.when((at >= 1) & (leaving < AH))
        def _():
            states = absorb([(load(leaving, part), part, ((2 * rows, rows, False),)) for part in wholes], leaving)
            for part, state in zip(wholes, states):
                store(leaving, part, state)
            arrived(NEAR, leaving, True)
            arrived(FAR, leaving, True)
            states = absorb([
                (load(leaving, part), part, ((rows, rows, False), (3 * rows, rows, False))) for part in wholes
            ], leaving)
            for part, (_, total, mixed) in zip(wholes, states):
                emit(leaving, part, mixed / total)

        @pl.when(entering < AH)
        def _():
            states = absorb([(None, part, (
                (part[0], rows - part[0], False), (WINDOW, part[0] + part[1], True)
            )) for part in halves], entering)
            for part, state in zip(halves, states):
                store(entering, part, state)

        done = at - final_lag

        @pl.when((done >= 0) & (done < moved))
        def _():
            @pl.when(upper == 1)
            def _():
                received(FROM_BESIDE, done, answer)

            @pl.when(plane >= 1)
            def _():
                received(FROM_BEHIND, done, answer)

            for part in halves:
                span = slice(part[0], part[0] + part[1])
                here = own_mix[done, span, :], own_log[done, span, :]

                @pl.when(first & (upper == 0))
                def _():
                    emit(done, part, here[0])

                @pl.when(first & (upper == 1))
                def _():
                    emit(done, part, merged([here, take_back(BESIDE, done, part)])[0])

                @pl.when((plane >= 1) & (upper == 0))
                def _():
                    emit(done, part, merged([here, take_back(OUTER, done, part)])[0])

                @pl.when((plane >= 1) & (upper == 1))
                def _():
                    emit(done, part, merged([here, take_back(OUTER, done, part), take_back(BESIDE, done, part)])[0])

        joined = at - JOIN_LAG

        @pl.when((upper == 0) & (joined >= 0) & (joined < moved_next))
        def _():
            received(FROM_BESIDE_TOO, joined, answer)
            for part in halves:
                span = slice(part[0], part[0] + part[1])
                here = held_mix[joined % 4, span, :], held_log[joined % 4, span, :]
                put_back(OUTER, joined, part, *merged([here, take_back(BESIDE, joined, part)]))
            give_back(OUTER, joined, TO_AHEAD, FROM_BEHIND, me + 4)

        return carry

    lax.fori_loop(0, AH + 3, turn, 0)

    def finish(head, carry):
        here, ahead = head < moved, head < moved_next
        stays, stays_ahead = head >= moved, (head >= moved_next) & (me + 4 < n)
        sent(stays_ahead, TO_AHEAD, head, pair)
        sent(ahead, TO_AHEAD, head, answer)
        sent(here & (plane >= 1), TO_BEHIND, head, block)
        sent(stays, TO_BEHIND, head, pair)
        sent(stays, TO_BESIDE, head, pair)
        sent(here & (upper == 1), TO_BESIDE, head, block)
        sent(here & (upper == 0), TO_BESIDE, head, answer)
        sent(ahead & (upper == 0), TO_BESIDE_TOO, head, block)
        sent(ahead & (upper == 1), TO_BESIDE_TOO, head, answer)
        sent((odd == 0) | stays | (head < asked_beside), TO_TWIN, head, pair)
        return carry

    lax.fori_loop(0, AH, finish, 0)

    @pl.when(me >= 4)
    def _():
        doc_copy(OUTER, doc_hbm, twin).wait_send()

    @pl.when((upper == 1) | jnp.logical_not(last))
    def _():
        doc_copy(BESIDE, doc_hbm, twin).wait_send()


def local(query_rows, key_rows, value_rows, doc_start, n):
    rows = query_rows.shape[0]
    reach = WINDOW // rows + 2
    operands = [
        pltpu.with_memory_space_constraint(x, pltpu.HBM)
        for x in (doc_start.reshape(1, rows), query_rows, key_rows, value_rows)
    ]
    mix, log = (2, AH, rows, DH), (2, AH, 2, rows)
    return pl.pallas_call(
        functools.partial(kernel, n, rows),
        out_shape=pltpu.VMEM(query_rows.shape, jnp.bfloat16),
        in_specs=[pl.BlockSpec(memory_space=pltpu.HBM)] * 4,
        out_specs=pl.BlockSpec(memory_space=pltpu.VMEM),
        scratch_shapes=[
            pltpu.VMEM((AH, rows, DH), jnp.bfloat16),
            pltpu.VMEM(mix, jnp.bfloat16),
            pltpu.VMEM((AH, reach * rows, DH), jnp.bfloat16),
            pltpu.VMEM((AH, reach * rows, DH), jnp.bfloat16),
            pltpu.VMEM((3, 1, rows), jnp.int32),
            pltpu.VMEM((3, rows, DH), jnp.int32),
            pltpu.VMEM((2, rows, DH), jnp.float32),
            pltpu.VMEM((2, rows, DH), jnp.float32),
            pltpu.VMEM((2, rows, DH), jnp.float32),
            pltpu.VMEM((AH, rows, DH), jnp.float32),
            pltpu.VMEM((AH, rows, DH), jnp.float32),
            pltpu.VMEM((4, rows, DH), jnp.float32),
            pltpu.VMEM((4, rows, DH), jnp.float32),
            pltpu.VMEM(mix, jnp.bfloat16),
            pltpu.VMEM(log, jnp.float32),
            pltpu.VMEM(mix, jnp.bfloat16),
            pltpu.VMEM(log, jnp.float32),
            pltpu.SemaphoreType.DMA,
            pltpu.SemaphoreType.DMA((2,)),
            pltpu.SemaphoreType.DMA((2,)),
            pltpu.SemaphoreType.DMA((5, AH)),
            pltpu.SemaphoreType.DMA((6, AH)),
        ],
        compiler_params=pltpu.CompilerParams(
            collective_id=0, has_side_effects=True, vmem_limit_bytes=56 * 1024 * 1024
        ),
    )(*operands)


def solution(mesh):
    placed = (
        P(("grp", "seq"), None),
        P(("grp", "seq"), None),
        P(("grp", "seq"), None),
        P(("grp", "seq")),
    )
    return jax.shard_map(
        functools.partial(local, n=mesh.shape["seq"]),
        mesh=mesh, in_specs=placed, out_specs=P(("grp", "seq"), None), check_vma=False,
    )
```

```python
import functools
import math

import jax
import jax.numpy as jnp
from jax import lax
from jax.experimental import pallas as pl
from jax.experimental.pallas import tpu as pltpu
from jax.sharding import PartitionSpec as P

AH = 12
DH = 128
WINDOW = 2048
MESH = pl.DeviceIdType.MESH
HIDDEN = -1e30
KEYS_AHEAD = 9
JOIN_LAG = 3
FINAL_LAG = 2
KEYS_TURN = 2
BESIDE_AHEAD = 1
QUERIES_AHEAD = 3
PIECES = 4
OUTER, BESIDE = 0, 1
NEXT, ACROSS, NEAR, FAR, AFTER = 0, 1, 2, 3, 4
CUTS = 2
WIDE = 2
LANDING = (0, 2, 3, 1, 5)
FROM_BESIDE, FROM_BESIDE_TOO, FROM_BEHIND, FROM_AHEAD, FROM_TWIN, FROM_HERE = 0, 1, 2, 3, 4, 5
TO_AHEAD, TO_BEHIND, TO_BESIDE, TO_BESIDE_TOO, TO_TWIN = 0, 1, 2, 3, 4
KV_RECV = (FROM_BEHIND, FROM_BESIDE, FROM_TWIN, FROM_BESIDE_TOO, FROM_TWIN)
KV_SEND = (TO_AHEAD, TO_BESIDE, TO_TWIN, TO_BEHIND, TO_TWIN)


def kernel(n, rows, doc_hbm, q_hbm, k_hbm, v_hbm, out_ref,
           q_buf, asked, k_buf, v_buf, doc_buf, low, top_buf, sum_buf, mix_buf,
           own_mix, own_log, held_mix, held_log, sent_mix, sent_log, got_mix, got_log,
           doc_sem, doc_send, doc_recv, send_sem, recv_sem, piece_sem):
    group = lax.axis_index("grp")
    me = lax.axis_index("seq")
    planes = n // 4
    plane = me // 4
    upper = (me // 2) % 2
    odd = me % 2
    beside = me + 2 - 4 * upper
    twin = me + 1 - 2 * odd
    halves = [(at * (rows // CUTS), rows // CUTS) for at in range(CUTS)]
    wholes = [(at * (rows // WIDE), rows // WIDE) for at in range(WIDE)]
    sources = (k_hbm, v_hbm)
    buffers = (k_buf, v_buf)
    first = plane == 0
    last = plane == planes - 1

    moved = AH * (planes - plane) // planes
    moved_next = AH * (planes - 1 - plane) // planes
    asked_beside = upper * moved_next + (1 - upper) * moved

    def columns(ref, head):
        return ref.at[pl.ds(0, rows), pl.ds(pl.multiple_of(head * DH, DH), DH)]

    def slot(which, head, shard):
        return buffers[which].at[head, pl.ds(shard * rows, rows), :]

    def own_copies(head):
        pairs = [(q_hbm, q_buf.at[head])] + [(sources[w], slot(w, head, 4)) for w in (0, 1)]
        return [
            pltpu.make_async_copy(columns(source, head), target, recv_sem.at[FROM_HERE, head])
            for source, target in pairs
        ]

    def remote(source, target, send, recv, device):
        return pltpu.make_async_remote_copy(
            src_ref=source, dst_ref=target, send_sem=send, recv_sem=recv,
            device_id=(group, device), device_id_type=MESH,
        )

    block, pair, three, answer = rows, 2 * rows, 3 * rows, rows + 16

    def settle(sem, size):
        view = k_buf.at[0, pl.ds(0, size), :]
        pltpu.make_async_copy(view, view, sem).wait()

    def received(at, head, size):
        settle(recv_sem.at[at, head], size)

    def sent(condition, at, head, size):
        @pl.when(condition)
        def _():
            settle(send_sem.at[at, head], size)

    def begin(condition, kind, head, source_shard, device):
        @pl.when(condition)
        def _():
            for w in (0, 1):
                source = columns(sources[w], head) if source_shard is None else slot(w, head, source_shard)
                remote(source, slot(w, head, LANDING[kind]), send_sem.at[KV_SEND[kind], head],
                       recv_sem.at[KV_RECV[kind], head], device).start()

    def arrived(kind, head, condition):
        @pl.when(condition)
        def _():
            received(KV_RECV[kind], head, pair)

    piece = rows // PIECES

    def ask_behind_first():
        for at in range(PIECES):
            span = pl.ds(at * piece, piece)
            remote(q_hbm.at[span, pl.ds(0, DH)], asked.at[OUTER, 0, span, :], send_sem.at[TO_BEHIND, 0],
                   piece_sem.at[at], me - 4).start()

    def ask_behind(head):
        remote(columns(q_hbm, head), asked.at[OUTER, head], send_sem.at[TO_BEHIND, head],
               recv_sem.at[FROM_AHEAD, head], me - 4).start()

    def ask_beside(head, source, send, recv):
        remote(source, asked.at[BESIDE, head], send_sem.at[send, head], recv_sem.at[recv, head], beside).start()

    def doc_copy(way, source, device):
        return remote(source, doc_buf.at[1 + way], doc_send.at[way], doc_recv.at[way], device)

    def give_back(way, head, send, recv, device):
        for source, target in ((sent_mix, got_mix), (sent_log, got_log)):
            remote(source.at[way, head], target.at[way, head], send_sem.at[send, head],
                   recv_sem.at[recv, head], device).start()

    doc_own = pltpu.make_async_copy(doc_hbm, doc_buf.at[0], doc_sem)
    doc_own.start()
    barrier = pltpu.get_barrier_semaphore()
    pl.semaphore_signal(barrier, inc=1, device_id=(group, beside), device_id_type=MESH)
    pl.semaphore_signal(barrier, inc=1, device_id=(group, twin), device_id_type=MESH)

    @pl.when(me >= 4)
    def _():
        pl.semaphore_signal(barrier, inc=1, device_id=(group, me - 4), device_id_type=MESH)

    @pl.when(me + 4 < n)
    def _():
        pl.semaphore_signal(barrier, inc=1, device_id=(group, me + 4), device_id_type=MESH)

    def fetch(head, carry):
        for copy in own_copies(head):
            copy.start()
        return carry

    lax.fori_loop(0, AH, fetch, 0)

    peers = 2 + (me >= 4).astype(jnp.int32) + (me + 4 < n).astype(jnp.int32)
    pl.semaphore_wait(barrier, peers)

    def send_next(at):
        head = moved_next + at
        begin((me + 4 < n) & (head < AH), NEXT, head, None, me + 4)

    def send_beside(at):
        head = moved + at
        begin((upper == 0) & (head < AH), ACROSS, head, None, beside)

    def send_query(head):
        @pl.when((upper == 1) & (head < moved))
        def _():
            ask_beside(head, columns(q_hbm, head), TO_BESIDE, FROM_BESIDE)

    @pl.when(me >= 4)
    def _():
        doc_copy(OUTER, doc_hbm, me - 4).start()

    @pl.when(upper == 1)
    def _():
        doc_copy(BESIDE, doc_hbm, beside).start()

    for at in range(max(KEYS_AHEAD, BESIDE_AHEAD, QUERIES_AHEAD)):
        @pl.when((me >= 4) & (at < moved))
        def _():
            ask_behind(at) if at else ask_behind_first()

        if at < QUERIES_AHEAD:
            send_query(at)
        if at < BESIDE_AHEAD:
            send_beside(at)
        if at < KEYS_AHEAD:
            send_next(at)

    def opening(head, carry):
        @pl.when((me >= 4) & (head < moved) & (head >= max(KEYS_AHEAD, BESIDE_AHEAD, QUERIES_AHEAD)))
        def _():
            ask_behind(head)

        begin(odd == 0, NEAR, head, None, twin)
        begin((odd == 1) & (head < asked_beside), AFTER, head, None, twin)
        return carry

    lax.fori_loop(0, AH, opening, 0)

    row = lax.broadcasted_iota(jnp.int32, (rows, DH), 0)

    def column(values, count):
        return jnp.transpose(jnp.broadcast_to(values, (DH, count)))

    def set_low(at, distance):
        starts = column(doc_buf[at], rows)
        low[at] = jnp.maximum(starts - (me * rows - WINDOW), row + (1 + distance * rows))

    doc_own.wait()
    set_low(0, 0)

    def own_wait(head, condition):
        @pl.when(condition)
        def _():
            received(FROM_HERE, head, three)

    scale = math.log2(math.e) / math.sqrt(DH)

    def across(values, count):
        return values if count == DH else jnp.concatenate([values] * (count // DH), axis=1)

    def absorb(jobs, head, source=None):
        scored = []
        for state, part, spans in jobs:
            span = slice(part[0], part[0] + part[1])
            queries = q_buf[head, span, :] if source is None else asked[source, head, span, :]
            lowest = low[0 if source is None else 1 + source, span, :]
            every = []
            for start, count, upto in spans:
                scores = lax.dot_general(
                    queries, k_buf[head, pl.ds(start, count), :], (((1,), (1,)), ((), ())),
                    preferred_element_type=jnp.float32,
                )
                place = start + lax.broadcasted_iota(jnp.int32, (part[1], count), 1)
                allowed = place >= across(lowest, count)
                if upto:
                    query = part[0] + lax.broadcasted_iota(jnp.int32, (part[1], count), 0)
                    allowed = allowed & (place <= query + WINDOW)
                every.append(jnp.where(allowed, scores, HIDDEN))
            scored.append(every)
        results = []
        for (state, part, spans), every in zip(jobs, scored):
            largest = functools.reduce(jnp.maximum, [jnp.max(x, axis=1, keepdims=True) for x in every])
            largest = jnp.broadcast_to(largest, (part[1], DH))
            if state is not None:
                largest = jnp.maximum(largest, state[0])
            total = mixed = 0.0
            if state is not None:
                fade = jnp.exp2((state[0] - largest) * scale)
                total, mixed = state[1] * fade, state[2] * fade
            for (start, count, _), scores in zip(spans, every):
                powers = jnp.exp2((scores - across(largest, count)) * scale)
                total = total + jnp.broadcast_to(jnp.sum(powers, axis=1, keepdims=True), (part[1], DH))
                mixed = mixed + jnp.dot(
                    powers.astype(jnp.bfloat16), v_buf[head, pl.ds(start, count), :],
                    preferred_element_type=jnp.float32,
                )
            results.append((largest, total, mixed))
        return results

    def load(head, part):
        span = slice(part[0], part[0] + part[1])
        at = head % 2
        return top_buf[at, span, :], sum_buf[at, span, :], mix_buf[at, span, :]

    def store(head, part, state):
        span = slice(part[0], part[0] + part[1])
        at = head % 2
        top_buf[at, span, :] = state[0]
        sum_buf[at, span, :] = state[1]
        mix_buf[at, span, :] = state[2]

    def emit(head, part, values):
        span = slice(part[0], part[0] + part[1])
        out_ref[span, pl.ds(pl.multiple_of(head * DH, DH), DH)] = values.astype(jnp.bfloat16)

    def closed(state):
        largest, total, mixed = state
        return mixed / total, largest * scale + jnp.log2(total)

    def put_back(way, head, part, mixed, log):
        span = slice(part[0], part[0] + part[1])
        sent_mix[way, head, span, :] = mixed.astype(jnp.bfloat16)
        sent_log[way, head, :, span] = jnp.transpose(log)[0:2, :]

    def take_back(way, head, part):
        span = slice(part[0], part[0] + part[1])
        return got_mix[way, head, span, :].astype(jnp.float32), column(got_log[way, head, 0:1, span], part[1])

    def merged(pieces):
        largest = functools.reduce(jnp.maximum, [log for _, log in pieces])
        total = mixed = 0.0
        for values, log in pieces:
            weight = jnp.exp2(log - largest)
            total = total + weight
            mixed = mixed + values * weight
        return mixed / total, largest + jnp.log2(total)

    def beside_service(head):
        received(upper, head, block)
        start = pl.multiple_of((4 - odd) * rows, rows)
        states = absorb([(None, part, ((start, 2 * rows, False),)) for part in wholes], head, BESIDE)
        for part, state in zip(wholes, states):
            put_back(BESIDE, head, part, *closed(state))
        give_back(BESIDE, head, TO_BESIDE + upper, upper, beside)

    def outer_service(head, count):
        states = absorb([(None, part, ((WINDOW + part[0], count - part[0], False),)) for part in halves], head, OUTER)
        for part, state in zip(halves, states):
            span = slice(part[0], part[0] + part[1])
            mixed, log = closed(state)

            @pl.when(upper == 1)
            def _():
                put_back(OUTER, head, part, mixed, log)

            @pl.when(upper == 0)
            def _():
                held_mix[head % 4, span, :] = mixed
                held_log[head % 4, span, :] = log

    def own_part(head, start):
        states = absorb([(None, part, ((start, WINDOW + part[0] + part[1] - start, True),)) for part in halves], head)
        for part, state in zip(halves, states):
            span = slice(part[0], part[0] + part[1])
            mixed, log = closed(state)
            own_mix[head, span, :] = mixed
            own_log[head, span, :] = log

    final_lag = jnp.maximum(FINAL_LAG, AH - moved)

    def turn(at, carry):
        entering = moved + at
        leaving = entering - 1

        own_wait(at, at < moved)
        own_wait(moved + at, moved + at < AH)
        arrived(NEAR, at, (odd == 1) & (at < moved))
        arrived(AFTER, at, (odd == 0) & (at < asked_beside))

        @pl.when(entering < AH)
        def _():
            arrived(NEXT, entering, True)
            begin(upper == 1, ACROSS, entering, 0, beside)
            begin(odd == 1, FAR, entering, 0, twin)

        @pl.when((at == 0) & jnp.logical_not(last))
        def _():
            for part in range(PIECES):
                settle(piece_sem.at[part], piece)

                @pl.when(upper == 0)
                def _():
                    span = pl.ds(part * piece, piece)
                    remote(asked.at[OUTER, 0, span, :], asked.at[BESIDE, 0, span, :], send_sem.at[TO_BESIDE_TOO, 0],
                           recv_sem.at[FROM_BESIDE_TOO, 0], beside).start()

            doc_copy(OUTER, doc_hbm, twin).wait_recv()

            @pl.when(upper == 0)
            def _():
                doc_copy(BESIDE, doc_buf.at[1 + OUTER], beside).start()

            set_low(1 + OUTER, 4)

        @pl.when((at >= 1) & (at < moved_next))
        def _():
            received(FROM_AHEAD, at, block)

            @pl.when(upper == 0)
            def _():
                ask_beside(at, asked.at[OUTER, at], TO_BESIDE_TOO, FROM_BESIDE_TOO)

        served = at - upper

        @pl.when((served == 0) & (served < asked_beside))
        def _():
            doc_copy(BESIDE, doc_hbm, twin).wait_recv()
            set_low(1 + BESIDE, 2)

        @pl.when((served >= 0) & (served < asked_beside))
        def _():
            beside_service(served)

        @pl.when((at >= 1) & (leaving < AH))
        def _():
            arrived(ACROSS, leaving, True)
            begin(odd == 1, NEAR, leaving, 2, twin)
            begin(odd == 0, FAR, leaving, 2, twin)

        for extra in range(KEYS_TURN):
            send_next(KEYS_AHEAD + at * KEYS_TURN + extra)
        send_beside(at + BESIDE_AHEAD)
        send_query(at + QUERIES_AHEAD)

        @pl.when((at < moved_next) & (odd == 0))
        def _():
            outer_service(at, 2 * rows)

        @pl.when((at < moved_next) & (odd == 1))
        def _():
            outer_service(at, rows)

        @pl.when((at < moved_next) & (upper == 1))
        def _():
            give_back(OUTER, at, TO_AHEAD, FROM_BEHIND, me + 4)

        joined = at - JOIN_LAG

        @pl.when((upper == 0) & (joined >= 0) & (joined < moved_next))
        def _():
            received(FROM_BESIDE_TOO, joined, answer)
            for part in halves:
                span = slice(part[0], part[0] + part[1])
                here = held_mix[joined % 4, span, :], held_log[joined % 4, span, :]
                put_back(OUTER, joined, part, *merged([here, take_back(BESIDE, joined, part)]))
            give_back(OUTER, joined, TO_AHEAD, FROM_BEHIND, me + 4)

        @pl.when((at >= 1) & (leaving < AH))
        def _():
            states = absorb([(load(leaving, part), part, ((2 * rows, rows, False),)) for part in wholes], leaving)
            for part, state in zip(wholes, states):
                store(leaving, part, state)
            arrived(NEAR, leaving, True)
            arrived(FAR, leaving, True)
            states = absorb([
                (load(leaving, part), part, ((rows, rows, False), (3 * rows, rows, False))) for part in wholes
            ], leaving)
            for part, (_, total, mixed) in zip(wholes, states):
                emit(leaving, part, mixed / total)

        @pl.when(entering < AH)
        def _():
            states = absorb([(None, part, (
                (part[0], rows - part[0], False), (WINDOW, part[0] + part[1], True)
            )) for part in halves], entering)
            for part, state in zip(halves, states):
                store(entering, part, state)

        @pl.when((at < moved) & (odd == 0))
        def _():
            own_part(at, WINDOW)

        @pl.when((at < moved) & (odd == 1))
        def _():
            own_part(at, WINDOW - rows)

        done = at - final_lag

        @pl.when((done >= 0) & (done < moved))
        def _():
            @pl.when(upper == 1)
            def _():
                received(FROM_BESIDE, done, answer)

            @pl.when(plane >= 1)
            def _():
                received(FROM_BEHIND, done, answer)

            for part in halves:
                span = slice(part[0], part[0] + part[1])
                here = own_mix[done, span, :], own_log[done, span, :]

                @pl.when(first & (upper == 0))
                def _():
                    emit(done, part, here[0])

                @pl.when(first & (upper == 1))
                def _():
                    emit(done, part, merged([here, take_back(BESIDE, done, part)])[0])

                @pl.when((plane >= 1) & (upper == 0))
                def _():
                    emit(done, part, merged([here, take_back(OUTER, done, part)])[0])

                @pl.when((plane >= 1) & (upper == 1))
                def _():
                    emit(done, part, merged([here, take_back(OUTER, done, part), take_back(BESIDE, done, part)])[0])

        return carry

    lax.fori_loop(0, AH + 3, turn, 0)

    def finish(head, carry):
        here, ahead = head < moved, head < moved_next
        stays, stays_ahead = head >= moved, (head >= moved_next) & (me + 4 < n)
        sent(stays_ahead, TO_AHEAD, head, pair)
        sent(ahead, TO_AHEAD, head, answer)
        sent(here & (plane >= 1), TO_BEHIND, head, block)
        sent(stays, TO_BEHIND, head, pair)
        sent(stays, TO_BESIDE, head, pair)
        sent(here & (upper == 1), TO_BESIDE, head, block)
        sent(here & (upper == 0), TO_BESIDE, head, answer)
        sent(ahead & (upper == 0), TO_BESIDE_TOO, head, block)
        sent(ahead & (upper == 1), TO_BESIDE_TOO, head, answer)
        sent((odd == 0) | stays | (head < asked_beside), TO_TWIN, head, pair)
        return carry

    lax.fori_loop(0, AH, finish, 0)

    @pl.when(me >= 4)
    def _():
        doc_copy(OUTER, doc_hbm, twin).wait_send()

    @pl.when((upper == 1) | jnp.logical_not(last))
    def _():
        doc_copy(BESIDE, doc_hbm, twin).wait_send()


def local(query_rows, key_rows, value_rows, doc_start, n):
    rows = query_rows.shape[0]
    reach = WINDOW // rows + 2
    operands = [
        pltpu.with_memory_space_constraint(x, pltpu.HBM)
        for x in (doc_start.reshape(1, rows), query_rows, key_rows, value_rows)
    ]
    mix, log = (2, AH, rows, DH), (2, AH, 2, rows)
    return pl.pallas_call(
        functools.partial(kernel, n, rows),
        out_shape=pltpu.VMEM(query_rows.shape, jnp.bfloat16),
        in_specs=[pl.BlockSpec(memory_space=pltpu.HBM)] * 4,
        out_specs=pl.BlockSpec(memory_space=pltpu.VMEM),
        scratch_shapes=[
            pltpu.VMEM((AH, rows, DH), jnp.bfloat16),
            pltpu.VMEM(mix, jnp.bfloat16),
            pltpu.VMEM((AH, reach * rows, DH), jnp.bfloat16),
            pltpu.VMEM((AH, reach * rows, DH), jnp.bfloat16),
            pltpu.VMEM((3, 1, rows), jnp.int32),
            pltpu.VMEM((3, rows, DH), jnp.int32),
            pltpu.VMEM((2, rows, DH), jnp.float32),
            pltpu.VMEM((2, rows, DH), jnp.float32),
            pltpu.VMEM((2, rows, DH), jnp.float32),
            pltpu.VMEM((AH, rows, DH), jnp.float32),
            pltpu.VMEM((AH, rows, DH), jnp.float32),
            pltpu.VMEM((4, rows, DH), jnp.float32),
            pltpu.VMEM((4, rows, DH), jnp.float32),
            pltpu.VMEM(mix, jnp.bfloat16),
            pltpu.VMEM(log, jnp.float32),
            pltpu.VMEM(mix, jnp.bfloat16),
            pltpu.VMEM(log, jnp.float32),
            pltpu.SemaphoreType.DMA,
            pltpu.SemaphoreType.DMA((2,)),
            pltpu.SemaphoreType.DMA((2,)),
            pltpu.SemaphoreType.DMA((5, AH)),
            pltpu.SemaphoreType.DMA((6, AH)),
            pltpu.SemaphoreType.DMA((PIECES,)),
        ],
        compiler_params=pltpu.CompilerParams(
            collective_id=0, has_side_effects=True, vmem_limit_bytes=56 * 1024 * 1024
        ),
    )(*operands)


def solution(mesh):
    placed = (
        P(("grp", "seq"), None),
        P(("grp", "seq"), None),
        P(("grp", "seq"), None),
        P(("grp", "seq")),
    )
    return jax.shard_map(
        functools.partial(local, n=mesh.shape["seq"]),
        mesh=mesh, in_specs=placed, out_specs=P(("grp", "seq"), None), check_vma=False,
    )
```

```python
import functools
import math

import jax
import jax.numpy as jnp
from jax import lax
from jax.experimental import pallas as pl
from jax.experimental.pallas import tpu as pltpu
from jax.sharding import PartitionSpec as P

AH = 12
DH = 128
WINDOW = 2048
MESH = pl.DeviceIdType.MESH
HIDDEN = -1e30
KEYS_AHEAD = 9
JOIN_LAG = 3
FINAL_LAG = 2
KEYS_TURN = 2
BESIDE_AHEAD = 2
QUERIES_AHEAD = 3
PIECES = 4
OUTER, BESIDE = 0, 1
NEXT, ACROSS, NEAR, FAR, AFTER = 0, 1, 2, 3, 4
CUTS = 2
WIDE = 2
LANDING = (0, 2, 3, 1, 5)
FROM_BESIDE, FROM_BESIDE_TOO, FROM_BEHIND, FROM_AHEAD, FROM_TWIN, FROM_HERE = 0, 1, 2, 3, 4, 5
TO_AHEAD, TO_BEHIND, TO_BESIDE, TO_BESIDE_TOO, TO_TWIN = 0, 1, 2, 3, 4
KV_RECV = (FROM_BEHIND, FROM_BESIDE, FROM_TWIN, FROM_BESIDE_TOO, FROM_TWIN)
KV_SEND = (TO_AHEAD, TO_BESIDE, TO_TWIN, TO_BEHIND, TO_TWIN)


def kernel(n, rows, doc_hbm, q_hbm, k_hbm, v_hbm, out_ref,
           q_buf, asked, k_buf, v_buf, doc_buf, low, top_buf, sum_buf, mix_buf,
           own_mix, own_log, held_mix, held_log, sent_mix, sent_log, got_mix, got_log,
           doc_sem, doc_send, doc_recv, send_sem, recv_sem, piece_sem):
    group = lax.axis_index("grp")
    me = lax.axis_index("seq")
    planes = n // 4
    plane = me // 4
    upper = (me // 2) % 2
    odd = me % 2
    beside = me + 2 - 4 * upper
    twin = me + 1 - 2 * odd
    halves = [(at * (rows // CUTS), rows // CUTS) for at in range(CUTS)]
    wholes = [(at * (rows // WIDE), rows // WIDE) for at in range(WIDE)]
    sources = (k_hbm, v_hbm)
    buffers = (k_buf, v_buf)
    first = plane == 0
    last = plane == planes - 1

    moved = AH * (planes - plane) // planes
    moved_next = AH * (planes - 1 - plane) // planes
    asked_beside = upper * moved_next + (1 - upper) * moved

    def columns(ref, head):
        return ref.at[pl.ds(0, rows), pl.ds(pl.multiple_of(head * DH, DH), DH)]

    def slot(which, head, shard):
        return buffers[which].at[head, pl.ds(shard * rows, rows), :]

    def own_copies(head):
        pairs = [(q_hbm, q_buf.at[head])] + [(sources[w], slot(w, head, 4)) for w in (0, 1)]
        return [
            pltpu.make_async_copy(columns(source, head), target, recv_sem.at[FROM_HERE, head])
            for source, target in pairs
        ]

    def remote(source, target, send, recv, device):
        return pltpu.make_async_remote_copy(
            src_ref=source, dst_ref=target, send_sem=send, recv_sem=recv,
            device_id=(group, device), device_id_type=MESH,
        )

    block, pair, three, answer = rows, 2 * rows, 3 * rows, rows + 16

    def settle(sem, size):
        view = k_buf.at[0, pl.ds(0, size), :]
        pltpu.make_async_copy(view, view, sem).wait()

    def received(at, head, size):
        settle(recv_sem.at[at, head], size)

    def sent(condition, at, head, size):
        @pl.when(condition)
        def _():
            settle(send_sem.at[at, head], size)

    def begin(condition, kind, head, source_shard, device):
        @pl.when(condition)
        def _():
            for w in (0, 1):
                source = columns(sources[w], head) if source_shard is None else slot(w, head, source_shard)
                remote(source, slot(w, head, LANDING[kind]), send_sem.at[KV_SEND[kind], head],
                       recv_sem.at[KV_RECV[kind], head], device).start()

    def arrived(kind, head, condition):
        @pl.when(condition)
        def _():
            received(KV_RECV[kind], head, pair)

    piece = rows // PIECES

    def ask_behind_first():
        for at in range(PIECES):
            span = pl.ds(at * piece, piece)
            remote(q_hbm.at[span, pl.ds(0, DH)], asked.at[OUTER, 0, span, :], send_sem.at[TO_BEHIND, 0],
                   piece_sem.at[at], me - 4).start()

    def ask_behind(head):
        remote(columns(q_hbm, head), asked.at[OUTER, head], send_sem.at[TO_BEHIND, head],
               recv_sem.at[FROM_AHEAD, head], me - 4).start()

    def ask_beside(head, source, send, recv):
        remote(source, asked.at[BESIDE, head], send_sem.at[send, head], recv_sem.at[recv, head], beside).start()

    def doc_copy(way, source, device):
        return remote(source, doc_buf.at[1 + way], doc_send.at[way], doc_recv.at[way], device)

    def give_back(way, head, send, recv, device):
        for source, target in ((sent_mix, got_mix), (sent_log, got_log)):
            remote(source.at[way, head], target.at[way, head], send_sem.at[send, head],
                   recv_sem.at[recv, head], device).start()

    doc_own = pltpu.make_async_copy(doc_hbm, doc_buf.at[0], doc_sem)
    doc_own.start()
    barrier = pltpu.get_barrier_semaphore()
    pl.semaphore_signal(barrier, inc=1, device_id=(group, beside), device_id_type=MESH)
    pl.semaphore_signal(barrier, inc=1, device_id=(group, twin), device_id_type=MESH)

    @pl.when(me >= 4)
    def _():
        pl.semaphore_signal(barrier, inc=1, device_id=(group, me - 4), device_id_type=MESH)

    @pl.when(me + 4 < n)
    def _():
        pl.semaphore_signal(barrier, inc=1, device_id=(group, me + 4), device_id_type=MESH)

    def fetch(head, carry):
        for copy in own_copies(head):
            copy.start()
        return carry

    lax.fori_loop(0, AH, fetch, 0)

    peers = 2 + (me >= 4).astype(jnp.int32) + (me + 4 < n).astype(jnp.int32)
    pl.semaphore_wait(barrier, peers)

    def send_next(at):
        head = moved_next + at
        begin((me + 4 < n) & (head < AH), NEXT, head, None, me + 4)

    def send_beside(at):
        head = moved + at
        begin((upper == 0) & (head < AH), ACROSS, head, None, beside)

    def send_query(head):
        @pl.when((upper == 1) & (head < moved))
        def _():
            ask_beside(head, columns(q_hbm, head), TO_BESIDE, FROM_BESIDE)

    @pl.when(me >= 4)
    def _():
        doc_copy(OUTER, doc_hbm, me - 4).start()

    @pl.when(upper == 1)
    def _():
        doc_copy(BESIDE, doc_hbm, beside).start()

    for at in range(max(KEYS_AHEAD, BESIDE_AHEAD, QUERIES_AHEAD)):
        @pl.when((me >= 4) & (at < moved))
        def _():
            ask_behind(at) if at else ask_behind_first()

        if at < QUERIES_AHEAD:
            send_query(at)
        if at < BESIDE_AHEAD:
            send_beside(at)
        if at < KEYS_AHEAD:
            send_next(at)

    def opening(head, carry):
        @pl.when((me >= 4) & (head < moved) & (head >= max(KEYS_AHEAD, BESIDE_AHEAD, QUERIES_AHEAD)))
        def _():
            ask_behind(head)

        begin(odd == 0, NEAR, head, None, twin)
        begin((odd == 1) & (head < asked_beside), AFTER, head, None, twin)
        return carry

    lax.fori_loop(0, AH, opening, 0)

    row = lax.broadcasted_iota(jnp.int32, (rows, DH), 0)

    def column(values, count):
        return jnp.transpose(jnp.broadcast_to(values, (DH, count)))

    def set_low(at, distance):
        starts = column(doc_buf[at], rows)
        low[at] = jnp.maximum(starts - (me * rows - WINDOW), row + (1 + distance * rows))

    doc_own.wait()
    set_low(0, 0)

    def own_wait(head, condition):
        @pl.when(condition)
        def _():
            received(FROM_HERE, head, three)

    scale = math.log2(math.e) / math.sqrt(DH)

    def across(values, count):
        return values if count == DH else jnp.concatenate([values] * (count // DH), axis=1)

    def absorb(jobs, head, source=None):
        scored = []
        for state, part, spans in jobs:
            span = slice(part[0], part[0] + part[1])
            queries = q_buf[head, span, :] if source is None else asked[source, head, span, :]
            lowest = low[0 if source is None else 1 + source, span, :]
            every = []
            for start, count, upto in spans:
                scores = lax.dot_general(
                    queries, k_buf[head, pl.ds(start, count), :], (((1,), (1,)), ((), ())),
                    preferred_element_type=jnp.float32,
                )
                place = start + lax.broadcasted_iota(jnp.int32, (part[1], count), 1)
                allowed = place >= across(lowest, count)
                if upto:
                    query = part[0] + lax.broadcasted_iota(jnp.int32, (part[1], count), 0)
                    allowed = allowed & (place <= query + WINDOW)
                every.append(jnp.where(allowed, scores, HIDDEN))
            scored.append(every)
        results = []
        for (state, part, spans), every in zip(jobs, scored):
            largest = functools.reduce(jnp.maximum, [jnp.max(x, axis=1, keepdims=True) for x in every])
            largest = jnp.broadcast_to(largest, (part[1], DH))
            if state is not None:
                largest = jnp.maximum(largest, state[0])
            total = mixed = 0.0
            if state is not None:
                fade = jnp.exp2((state[0] - largest) * scale)
                total, mixed = state[1] * fade, state[2] * fade
            for (start, count, _), scores in zip(spans, every):
                powers = jnp.exp2((scores - across(largest, count)) * scale)
                total = total + jnp.broadcast_to(jnp.sum(powers, axis=1, keepdims=True), (part[1], DH))
                mixed = mixed + jnp.dot(
                    powers.astype(jnp.bfloat16), v_buf[head, pl.ds(start, count), :],
                    preferred_element_type=jnp.float32,
                )
            results.append((largest, total, mixed))
        return results

    def load(head, part):
        span = slice(part[0], part[0] + part[1])
        at = head % 2
        return top_buf[at, span, :], sum_buf[at, span, :], mix_buf[at, span, :]

    def store(head, part, state):
        span = slice(part[0], part[0] + part[1])
        at = head % 2
        top_buf[at, span, :] = state[0]
        sum_buf[at, span, :] = state[1]
        mix_buf[at, span, :] = state[2]

    def emit(head, part, values):
        span = slice(part[0], part[0] + part[1])
        out_ref[span, pl.ds(pl.multiple_of(head * DH, DH), DH)] = values.astype(jnp.bfloat16)

    def closed(state):
        largest, total, mixed = state
        return mixed / total, largest * scale + jnp.log2(total)

    def put_back(way, head, part, mixed, log):
        span = slice(part[0], part[0] + part[1])
        sent_mix[way, head, span, :] = mixed.astype(jnp.bfloat16)
        sent_log[way, head, :, span] = jnp.transpose(log)[0:2, :]

    def take_back(way, head, part):
        span = slice(part[0], part[0] + part[1])
        return got_mix[way, head, span, :].astype(jnp.float32), column(got_log[way, head, 0:1, span], part[1])

    def merged(pieces):
        largest = functools.reduce(jnp.maximum, [log for _, log in pieces])
        total = mixed = 0.0
        for values, log in pieces:
            weight = jnp.exp2(log - largest)
            total = total + weight
            mixed = mixed + values * weight
        return mixed / total, largest + jnp.log2(total)

    def beside_service(head):
        received(upper, head, block)
        start = pl.multiple_of((4 - odd) * rows, rows)
        states = absorb([(None, part, ((start, 2 * rows, False),)) for part in wholes], head, BESIDE)
        for part, state in zip(wholes, states):
            put_back(BESIDE, head, part, *closed(state))
        give_back(BESIDE, head, TO_BESIDE + upper, upper, beside)

    def outer_service(head, count):
        states = absorb([(None, part, ((WINDOW + part[0], count - part[0], False),)) for part in halves], head, OUTER)
        for part, state in zip(halves, states):
            span = slice(part[0], part[0] + part[1])
            mixed, log = closed(state)

            @pl.when(upper == 1)
            def _():
                put_back(OUTER, head, part, mixed, log)

            @pl.when(upper == 0)
            def _():
                held_mix[head % 4, span, :] = mixed
                held_log[head % 4, span, :] = log

    def own_part(head, start):
        states = absorb([(None, part, ((start, WINDOW + part[0] + part[1] - start, True),)) for part in halves], head)
        for part, state in zip(halves, states):
            span = slice(part[0], part[0] + part[1])
            mixed, log = closed(state)
            own_mix[head, span, :] = mixed
            own_log[head, span, :] = log

    final_lag = jnp.maximum(FINAL_LAG, AH - moved)

    def turn(at, carry):
        entering = moved + at
        leaving = entering - 1

        own_wait(at, at < moved)
        own_wait(moved + at, moved + at < AH)
        arrived(NEAR, at, (odd == 1) & (at < moved))
        arrived(AFTER, at, (odd == 0) & (at < asked_beside))

        @pl.when(entering < AH)
        def _():
            arrived(NEXT, entering, True)
            begin(upper == 1, ACROSS, entering, 0, beside)
            begin(odd == 1, FAR, entering, 0, twin)

        @pl.when((at == 0) & jnp.logical_not(last))
        def _():
            for part in range(PIECES):
                settle(piece_sem.at[part], piece)

                @pl.when(upper == 0)
                def _():
                    span = pl.ds(part * piece, piece)
                    remote(asked.at[OUTER, 0, span, :], asked.at[BESIDE, 0, span, :], send_sem.at[TO_BESIDE_TOO, 0],
                           recv_sem.at[FROM_BESIDE_TOO, 0], beside).start()

            doc_copy(OUTER, doc_hbm, twin).wait_recv()

            @pl.when(upper == 0)
            def _():
                doc_copy(BESIDE, doc_buf.at[1 + OUTER], beside).start()

            set_low(1 + OUTER, 4)

        @pl.when((at >= 1) & (at < moved_next))
        def _():
            received(FROM_AHEAD, at, block)

            @pl.when(upper == 0)
            def _():
                ask_beside(at, asked.at[OUTER, at], TO_BESIDE_TOO, FROM_BESIDE_TOO)

        served = at - upper

        @pl.when((served == 0) & (served < asked_beside))
        def _():
            doc_copy(BESIDE, doc_hbm, twin).wait_recv()
            set_low(1 + BESIDE, 2)

        @pl.when((served >= 0) & (served < asked_beside))
        def _():
            beside_service(served)

        @pl.when((at >= 1) & (leaving < AH))
        def _():
            arrived(ACROSS, leaving, True)
            begin(odd == 1, NEAR, leaving, 2, twin)
            begin(odd == 0, FAR, leaving, 2, twin)

        for extra in range(KEYS_TURN):
            send_next(KEYS_AHEAD + at * KEYS_TURN + extra)
        send_beside(at + BESIDE_AHEAD)
        send_query(at + QUERIES_AHEAD)

        @pl.when((at < moved_next) & (odd == 0))
        def _():
            outer_service(at, 2 * rows)

        @pl.when((at < moved_next) & (odd == 1))
        def _():
            outer_service(at, rows)

        @pl.when((at < moved_next) & (upper == 1))
        def _():
            give_back(OUTER, at, TO_AHEAD, FROM_BEHIND, me + 4)

        joined = at - JOIN_LAG

        @pl.when((upper == 0) & (joined >= 0) & (joined < moved_next))
        def _():
            received(FROM_BESIDE_TOO, joined, answer)
            for part in halves:
                span = slice(part[0], part[0] + part[1])
                here = held_mix[joined % 4, span, :], held_log[joined % 4, span, :]
                put_back(OUTER, joined, part, *merged([here, take_back(BESIDE, joined, part)]))
            give_back(OUTER, joined, TO_AHEAD, FROM_BEHIND, me + 4)

        done = at - final_lag

        @pl.when((done >= 0) & (done < moved))
        def _():
            @pl.when(upper == 1)
            def _():
                received(FROM_BESIDE, done, answer)

            @pl.when(plane >= 1)
            def _():
                received(FROM_BEHIND, done, answer)

            for part in halves:
                span = slice(part[0], part[0] + part[1])
                here = own_mix[done, span, :], own_log[done, span, :]

                @pl.when(first & (upper == 0))
                def _():
                    emit(done, part, here[0])

                @pl.when(first & (upper == 1))
                def _():
                    emit(done, part, merged([here, take_back(BESIDE, done, part)])[0])

                @pl.when((plane >= 1) & (upper == 0))
                def _():
                    emit(done, part, merged([here, take_back(OUTER, done, part)])[0])

                @pl.when((plane >= 1) & (upper == 1))
                def _():
                    emit(done, part, merged([here, take_back(OUTER, done, part), take_back(BESIDE, done, part)])[0])

        @pl.when((at >= 1) & (leaving < AH))
        def _():
            states = absorb([(load(leaving, part), part, ((2 * rows, rows, False),)) for part in wholes], leaving)
            for part, state in zip(wholes, states):
                store(leaving, part, state)
            arrived(NEAR, leaving, True)
            arrived(FAR, leaving, True)
            states = absorb([
                (load(leaving, part), part, ((rows, rows, False), (3 * rows, rows, False))) for part in wholes
            ], leaving)
            for part, (_, total, mixed) in zip(wholes, states):
                emit(leaving, part, mixed / total)

        @pl.when(entering < AH)
        def _():
            states = absorb([(None, part, (
                (part[0], rows - part[0], False), (WINDOW, part[0] + part[1], True)
            )) for part in halves], entering)
            for part, state in zip(halves, states):
                store(entering, part, state)

        @pl.when((at < moved) & (odd == 0))
        def _():
            own_part(at, WINDOW)

        @pl.when((at < moved) & (odd == 1))
        def _():
            own_part(at, WINDOW - rows)

        return carry

    lax.fori_loop(0, AH + 3, turn, 0)

    def finish(head, carry):
        here, ahead = head < moved, head < moved_next
        stays, stays_ahead = head >= moved, (head >= moved_next) & (me + 4 < n)
        sent(stays_ahead, TO_AHEAD, head, pair)
        sent(ahead, TO_AHEAD, head, answer)
        sent(here & (plane >= 1), TO_BEHIND, head, block)
        sent(stays, TO_BEHIND, head, pair)
        sent(stays, TO_BESIDE, head, pair)
        sent(here & (upper == 1), TO_BESIDE, head, block)
        sent(here & (upper == 0), TO_BESIDE, head, answer)
        sent(ahead & (upper == 0), TO_BESIDE_TOO, head, block)
        sent(ahead & (upper == 1), TO_BESIDE_TOO, head, answer)
        sent((odd == 0) | stays | (head < asked_beside), TO_TWIN, head, pair)
        return carry

    lax.fori_loop(0, AH, finish, 0)

    @pl.when(me >= 4)
    def _():
        doc_copy(OUTER, doc_hbm, twin).wait_send()

    @pl.when((upper == 1) | jnp.logical_not(last))
    def _():
        doc_copy(BESIDE, doc_hbm, twin).wait_send()


def local(query_rows, key_rows, value_rows, doc_start, n):
    rows = query_rows.shape[0]
    reach = WINDOW // rows + 2
    operands = [
        pltpu.with_memory_space_constraint(x, pltpu.HBM)
        for x in (doc_start.reshape(1, rows), query_rows, key_rows, value_rows)
    ]
    mix, log = (2, AH, rows, DH), (2, AH, 2, rows)
    return pl.pallas_call(
        functools.partial(kernel, n, rows),
        out_shape=pltpu.VMEM(query_rows.shape, jnp.bfloat16),
        in_specs=[pl.BlockSpec(memory_space=pltpu.HBM)] * 4,
        out_specs=pl.BlockSpec(memory_space=pltpu.VMEM),
        scratch_shapes=[
            pltpu.VMEM((AH, rows, DH), jnp.bfloat16),
            pltpu.VMEM(mix, jnp.bfloat16),
            pltpu.VMEM((AH, reach * rows, DH), jnp.bfloat16),
            pltpu.VMEM((AH, reach * rows, DH), jnp.bfloat16),
            pltpu.VMEM((3, 1, rows), jnp.int32),
            pltpu.VMEM((3, rows, DH), jnp.int32),
            pltpu.VMEM((2, rows, DH), jnp.float32),
            pltpu.VMEM((2, rows, DH), jnp.float32),
            pltpu.VMEM((2, rows, DH), jnp.float32),
            pltpu.VMEM((AH, rows, DH), jnp.float32),
            pltpu.VMEM((AH, rows, DH), jnp.float32),
            pltpu.VMEM((4, rows, DH), jnp.float32),
            pltpu.VMEM((4, rows, DH), jnp.float32),
            pltpu.VMEM(mix, jnp.bfloat16),
            pltpu.VMEM(log, jnp.float32),
            pltpu.VMEM(mix, jnp.bfloat16),
            pltpu.VMEM(log, jnp.float32),
            pltpu.SemaphoreType.DMA,
            pltpu.SemaphoreType.DMA((2,)),
            pltpu.SemaphoreType.DMA((2,)),
            pltpu.SemaphoreType.DMA((5, AH)),
            pltpu.SemaphoreType.DMA((6, AH)),
            pltpu.SemaphoreType.DMA((PIECES,)),
        ],
        compiler_params=pltpu.CompilerParams(
            collective_id=0, has_side_effects=True, vmem_limit_bytes=56 * 1024 * 1024
        ),
    )(*operands)


def solution(mesh):
    placed = (
        P(("grp", "seq"), None),
        P(("grp", "seq"), None),
        P(("grp", "seq"), None),
        P(("grp", "seq")),
    )
    return jax.shard_map(
        functools.partial(local, n=mesh.shape["seq"]),
        mesh=mesh, in_specs=placed, out_specs=P(("grp", "seq"), None), check_vma=False,
    )
```

```python
import functools
import math

import jax
import jax.numpy as jnp
from jax import lax
from jax.experimental import pallas as pl
from jax.experimental.pallas import tpu as pltpu
from jax.sharding import PartitionSpec as P

AH = 12
DH = 128
WINDOW = 2048
MESH = pl.DeviceIdType.MESH
HIDDEN = -1e30
KEYS_AHEAD = 9
JOIN_LAG = 3
FINAL_LAG = 2
SETTLE_LAG = 5
KEYS_TURN = 2
BESIDE_AHEAD = 2
QUERIES_AHEAD = 3
PIECES = 4
OUTER, BESIDE = 0, 1
NEXT, ACROSS, NEAR, FAR, AFTER = 0, 1, 2, 3, 4
CUTS = 2
WIDE = 2
LANDING = (0, 2, 3, 1, 5)
FROM_BESIDE, FROM_BESIDE_TOO, FROM_BEHIND, FROM_AHEAD, FROM_TWIN, FROM_HERE = 0, 1, 2, 3, 4, 5
TO_AHEAD, TO_BEHIND, TO_BESIDE, TO_BESIDE_TOO, TO_TWIN = 0, 1, 2, 3, 4
KV_RECV = (FROM_BEHIND, FROM_BESIDE, FROM_TWIN, FROM_BESIDE_TOO, FROM_TWIN)
KV_SEND = (TO_AHEAD, TO_BESIDE, TO_TWIN, TO_BEHIND, TO_TWIN)


def kernel(n, rows, doc_hbm, q_hbm, k_hbm, v_hbm, out_ref,
           q_buf, asked, k_buf, v_buf, doc_buf, low, top_buf, sum_buf, mix_buf,
           own_mix, own_log, held_mix, held_log, sent_mix, sent_log, got_mix, got_log,
           doc_sem, doc_send, doc_recv, send_sem, recv_sem, piece_sem):
    group = lax.axis_index("grp")
    me = lax.axis_index("seq")
    planes = n // 4
    plane = me // 4
    upper = (me // 2) % 2
    odd = me % 2
    beside = me + 2 - 4 * upper
    twin = me + 1 - 2 * odd
    halves = [(at * (rows // CUTS), rows // CUTS) for at in range(CUTS)]
    wholes = [(at * (rows // WIDE), rows // WIDE) for at in range(WIDE)]
    sources = (k_hbm, v_hbm)
    buffers = (k_buf, v_buf)
    first = plane == 0
    last = plane == planes - 1

    moved = AH * (planes - plane) // planes
    moved_next = AH * (planes - 1 - plane) // planes
    asked_beside = upper * moved_next + (1 - upper) * moved

    def columns(ref, head):
        return ref.at[pl.ds(0, rows), pl.ds(pl.multiple_of(head * DH, DH), DH)]

    def slot(which, head, shard):
        return buffers[which].at[head, pl.ds(shard * rows, rows), :]

    def own_copies(head):
        pairs = [(q_hbm, q_buf.at[head])] + [(sources[w], slot(w, head, 4)) for w in (0, 1)]
        return [
            pltpu.make_async_copy(columns(source, head), target, recv_sem.at[FROM_HERE, head])
            for source, target in pairs
        ]

    def remote(source, target, send, recv, device):
        return pltpu.make_async_remote_copy(
            src_ref=source, dst_ref=target, send_sem=send, recv_sem=recv,
            device_id=(group, device), device_id_type=MESH,
        )

    block, pair, three, answer = rows, 2 * rows, 3 * rows, rows + 16

    def settle(sem, size):
        view = k_buf.at[0, pl.ds(0, size), :]
        pltpu.make_async_copy(view, view, sem).wait()

    def received(at, head, size):
        settle(recv_sem.at[at, head], size)

    def sent(condition, at, head, size):
        @pl.when(condition)
        def _():
            settle(send_sem.at[at, head], size)

    def begin(condition, kind, head, source_shard, device):
        @pl.when(condition)
        def _():
            for w in (0, 1):
                source = columns(sources[w], head) if source_shard is None else slot(w, head, source_shard)
                remote(source, slot(w, head, LANDING[kind]), send_sem.at[KV_SEND[kind], head],
                       recv_sem.at[KV_RECV[kind], head], device).start()

    def arrived(kind, head, condition):
        @pl.when(condition)
        def _():
            received(KV_RECV[kind], head, pair)

    piece = rows // PIECES

    def ask_behind_first():
        for at in range(PIECES):
            span = pl.ds(at * piece, piece)
            remote(q_hbm.at[span, pl.ds(0, DH)], asked.at[OUTER, 0, span, :], send_sem.at[TO_BEHIND, 0],
                   piece_sem.at[at], me - 4).start()

    def ask_behind(head):
        remote(columns(q_hbm, head), asked.at[OUTER, head], send_sem.at[TO_BEHIND, head],
               recv_sem.at[FROM_AHEAD, head], me - 4).start()

    def ask_beside(head, source, send, recv):
        remote(source, asked.at[BESIDE, head], send_sem.at[send, head], recv_sem.at[recv, head], beside).start()

    def doc_copy(way, source, device):
        return remote(source, doc_buf.at[1 + way], doc_send.at[way], doc_recv.at[way], device)

    def give_back(way, head, send, recv, device):
        for source, target in ((sent_mix, got_mix), (sent_log, got_log)):
            remote(source.at[way, head], target.at[way, head], send_sem.at[send, head],
                   recv_sem.at[recv, head], device).start()

    doc_own = pltpu.make_async_copy(doc_hbm, doc_buf.at[0], doc_sem)
    doc_own.start()
    barrier = pltpu.get_barrier_semaphore()
    pl.semaphore_signal(barrier, inc=1, device_id=(group, beside), device_id_type=MESH)
    pl.semaphore_signal(barrier, inc=1, device_id=(group, twin), device_id_type=MESH)

    @pl.when(me >= 4)
    def _():
        pl.semaphore_signal(barrier, inc=1, device_id=(group, me - 4), device_id_type=MESH)

    @pl.when(me + 4 < n)
    def _():
        pl.semaphore_signal(barrier, inc=1, device_id=(group, me + 4), device_id_type=MESH)

    def fetch(head, carry):
        for copy in own_copies(head):
            copy.start()
        return carry

    lax.fori_loop(0, AH, fetch, 0)

    peers = 2 + (me >= 4).astype(jnp.int32) + (me + 4 < n).astype(jnp.int32)
    pl.semaphore_wait(barrier, peers)

    def send_next(at):
        head = moved_next + at
        begin((me + 4 < n) & (head < AH), NEXT, head, None, me + 4)

    def send_beside(at):
        head = moved + at
        begin((upper == 0) & (head < AH), ACROSS, head, None, beside)

    def send_query(head):
        @pl.when((upper == 1) & (head < moved))
        def _():
            ask_beside(head, columns(q_hbm, head), TO_BESIDE, FROM_BESIDE)

    @pl.when(me >= 4)
    def _():
        doc_copy(OUTER, doc_hbm, me - 4).start()

    @pl.when(upper == 1)
    def _():
        doc_copy(BESIDE, doc_hbm, beside).start()

    for at in range(max(KEYS_AHEAD, BESIDE_AHEAD, QUERIES_AHEAD)):
        @pl.when((me >= 4) & (at < moved))
        def _():
            ask_behind(at) if at else ask_behind_first()

        if at < QUERIES_AHEAD:
            send_query(at)
        if at < BESIDE_AHEAD:
            send_beside(at)
        if at < KEYS_AHEAD:
            send_next(at)

    def opening(head, carry):
        @pl.when((me >= 4) & (head < moved) & (head >= max(KEYS_AHEAD, BESIDE_AHEAD, QUERIES_AHEAD)))
        def _():
            ask_behind(head)

        begin(odd == 0, NEAR, head, None, twin)
        begin((odd == 1) & (head < asked_beside), AFTER, head, None, twin)
        return carry

    lax.fori_loop(0, AH, opening, 0)

    row = lax.broadcasted_iota(jnp.int32, (rows, DH), 0)

    def column(values, count):
        return jnp.transpose(jnp.broadcast_to(values, (DH, count)))

    def set_low(at, distance):
        starts = column(doc_buf[at], rows)
        low[at] = jnp.maximum(starts - (me * rows - WINDOW), row + (1 + distance * rows))

    doc_own.wait()
    set_low(0, 0)

    def own_wait(head, condition):
        @pl.when(condition)
        def _():
            received(FROM_HERE, head, three)

    scale = math.log2(math.e) / math.sqrt(DH)

    def across(values, count):
        return values if count == DH else jnp.concatenate([values] * (count // DH), axis=1)

    def absorb(jobs, head, source=None):
        scored = []
        for state, part, spans in jobs:
            span = slice(part[0], part[0] + part[1])
            queries = q_buf[head, span, :] if source is None else asked[source, head, span, :]
            lowest = low[0 if source is None else 1 + source, span, :]
            every = []
            for start, count, upto in spans:
                scores = lax.dot_general(
                    queries, k_buf[head, pl.ds(start, count), :], (((1,), (1,)), ((), ())),
                    preferred_element_type=jnp.float32,
                )
                place = start + lax.broadcasted_iota(jnp.int32, (part[1], count), 1)
                allowed = place >= across(lowest, count)
                if upto:
                    query = part[0] + lax.broadcasted_iota(jnp.int32, (part[1], count), 0)
                    allowed = allowed & (place <= query + WINDOW)
                every.append(jnp.where(allowed, scores, HIDDEN))
            scored.append(every)
        results = []
        for (state, part, spans), every in zip(jobs, scored):
            largest = functools.reduce(jnp.maximum, [jnp.max(x, axis=1, keepdims=True) for x in every])
            largest = jnp.broadcast_to(largest, (part[1], DH))
            if state is not None:
                largest = jnp.maximum(largest, state[0])
            total = mixed = 0.0
            if state is not None:
                fade = jnp.exp2((state[0] - largest) * scale)
                total, mixed = state[1] * fade, state[2] * fade
            for (start, count, _), scores in zip(spans, every):
                powers = jnp.exp2((scores - across(largest, count)) * scale)
                total = total + jnp.broadcast_to(jnp.sum(powers, axis=1, keepdims=True), (part[1], DH))
                mixed = mixed + jnp.dot(
                    powers.astype(jnp.bfloat16), v_buf[head, pl.ds(start, count), :],
                    preferred_element_type=jnp.float32,
                )
            results.append((largest, total, mixed))
        return results

    def load(head, part):
        span = slice(part[0], part[0] + part[1])
        at = head % 2
        return top_buf[at, span, :], sum_buf[at, span, :], mix_buf[at, span, :]

    def store(head, part, state):
        span = slice(part[0], part[0] + part[1])
        at = head % 2
        top_buf[at, span, :] = state[0]
        sum_buf[at, span, :] = state[1]
        mix_buf[at, span, :] = state[2]

    def emit(head, part, values):
        span = slice(part[0], part[0] + part[1])
        out_ref[span, pl.ds(pl.multiple_of(head * DH, DH), DH)] = values.astype(jnp.bfloat16)

    def closed(state):
        largest, total, mixed = state
        return mixed / total, largest * scale + jnp.log2(total)

    def put_back(way, head, part, mixed, log):
        span = slice(part[0], part[0] + part[1])
        sent_mix[way, head, span, :] = mixed.astype(jnp.bfloat16)
        sent_log[way, head, :, span] = jnp.transpose(log)[0:2, :]

    def take_back(way, head, part):
        span = slice(part[0], part[0] + part[1])
        return got_mix[way, head, span, :].astype(jnp.float32), column(got_log[way, head, 0:1, span], part[1])

    def merged(pieces):
        largest = functools.reduce(jnp.maximum, [log for _, log in pieces])
        total = mixed = 0.0
        for values, log in pieces:
            weight = jnp.exp2(log - largest)
            total = total + weight
            mixed = mixed + values * weight
        return mixed / total, largest + jnp.log2(total)

    def beside_service(head):
        received(upper, head, block)
        start = pl.multiple_of((4 - odd) * rows, rows)
        states = absorb([(None, part, ((start, 2 * rows, False),)) for part in wholes], head, BESIDE)
        for part, state in zip(wholes, states):
            put_back(BESIDE, head, part, *closed(state))
        give_back(BESIDE, head, TO_BESIDE + upper, upper, beside)

    def outer_service(head, count):
        states = absorb([(None, part, ((WINDOW + part[0], count - part[0], False),)) for part in halves], head, OUTER)
        for part, state in zip(halves, states):
            span = slice(part[0], part[0] + part[1])
            mixed, log = closed(state)

            @pl.when(upper == 1)
            def _():
                put_back(OUTER, head, part, mixed, log)

            @pl.when(upper == 0)
            def _():
                held_mix[head % 4, span, :] = mixed
                held_log[head % 4, span, :] = log

    def own_part(head, start):
        states = absorb([(None, part, ((start, WINDOW + part[0] + part[1] - start, True),)) for part in halves], head)
        for part, state in zip(halves, states):
            span = slice(part[0], part[0] + part[1])
            mixed, log = closed(state)
            own_mix[head, span, :] = mixed
            own_log[head, span, :] = log

    final_lag = jnp.maximum(FINAL_LAG, AH - moved)

    def finish(head, carry):
        here, ahead = head < moved, head < moved_next
        stays, stays_ahead = head >= moved, (head >= moved_next) & (me + 4 < n)
        sent(stays_ahead, TO_AHEAD, head, pair)
        sent(ahead, TO_AHEAD, head, answer)
        sent(here & (plane >= 1), TO_BEHIND, head, block)
        sent(stays, TO_BEHIND, head, pair)
        sent(stays, TO_BESIDE, head, pair)
        sent(here & (upper == 1), TO_BESIDE, head, block)
        sent(here & (upper == 0), TO_BESIDE, head, answer)
        sent(ahead & (upper == 0), TO_BESIDE_TOO, head, block)
        sent(ahead & (upper == 1), TO_BESIDE_TOO, head, answer)
        sent((odd == 0) | stays | (head < asked_beside), TO_TWIN, head, pair)
        return carry

    def turn(at, carry):
        entering = moved + at
        leaving = entering - 1

        own_wait(at, at < moved)
        own_wait(moved + at, moved + at < AH)
        arrived(NEAR, at, (odd == 1) & (at < moved))
        arrived(AFTER, at, (odd == 0) & (at < asked_beside))

        @pl.when(entering < AH)
        def _():
            arrived(NEXT, entering, True)
            begin(upper == 1, ACROSS, entering, 0, beside)
            begin(odd == 1, FAR, entering, 0, twin)

        @pl.when((at == 0) & jnp.logical_not(last))
        def _():
            for part in range(PIECES):
                settle(piece_sem.at[part], piece)

                @pl.when(upper == 0)
                def _():
                    span = pl.ds(part * piece, piece)
                    remote(asked.at[OUTER, 0, span, :], asked.at[BESIDE, 0, span, :], send_sem.at[TO_BESIDE_TOO, 0],
                           recv_sem.at[FROM_BESIDE_TOO, 0], beside).start()

            doc_copy(OUTER, doc_hbm, twin).wait_recv()

            @pl.when(upper == 0)
            def _():
                doc_copy(BESIDE, doc_buf.at[1 + OUTER], beside).start()

            set_low(1 + OUTER, 4)

        @pl.when((at >= 1) & (at < moved_next))
        def _():
            received(FROM_AHEAD, at, block)

            @pl.when(upper == 0)
            def _():
                ask_beside(at, asked.at[OUTER, at], TO_BESIDE_TOO, FROM_BESIDE_TOO)

        served = at - upper

        @pl.when((served == 0) & (served < asked_beside))
        def _():
            doc_copy(BESIDE, doc_hbm, twin).wait_recv()
            set_low(1 + BESIDE, 2)

        @pl.when((served >= 0) & (served < asked_beside))
        def _():
            beside_service(served)

        @pl.when((at >= 1) & (leaving < AH))
        def _():
            arrived(ACROSS, leaving, True)
            begin(odd == 1, NEAR, leaving, 2, twin)
            begin(odd == 0, FAR, leaving, 2, twin)

        for extra in range(KEYS_TURN):
            send_next(KEYS_AHEAD + at * KEYS_TURN + extra)
        send_beside(at + BESIDE_AHEAD)
        send_query(at + QUERIES_AHEAD)

        @pl.when((at < moved_next) & (odd == 0))
        def _():
            outer_service(at, 2 * rows)

        @pl.when((at < moved_next) & (odd == 1))
        def _():
            outer_service(at, rows)

        @pl.when((at < moved_next) & (upper == 1))
        def _():
            give_back(OUTER, at, TO_AHEAD, FROM_BEHIND, me + 4)

        joined = at - JOIN_LAG

        @pl.when((upper == 0) & (joined >= 0) & (joined < moved_next))
        def _():
            received(FROM_BESIDE_TOO, joined, answer)
            for part in halves:
                span = slice(part[0], part[0] + part[1])
                here = held_mix[joined % 4, span, :], held_log[joined % 4, span, :]
                put_back(OUTER, joined, part, *merged([here, take_back(BESIDE, joined, part)]))
            give_back(OUTER, joined, TO_AHEAD, FROM_BEHIND, me + 4)

        @pl.when(at >= SETTLE_LAG)
        def _():
            finish(at - SETTLE_LAG, 0)

        done = at - final_lag

        @pl.when((done >= 0) & (done < moved))
        def _():
            @pl.when(upper == 1)
            def _():
                received(FROM_BESIDE, done, answer)

            @pl.when(plane >= 1)
            def _():
                received(FROM_BEHIND, done, answer)

            for part in halves:
                span = slice(part[0], part[0] + part[1])
                here = own_mix[done, span, :], own_log[done, span, :]

                @pl.when(first & (upper == 0))
                def _():
                    emit(done, part, here[0])

                @pl.when(first & (upper == 1))
                def _():
                    emit(done, part, merged([here, take_back(BESIDE, done, part)])[0])

                @pl.when((plane >= 1) & (upper == 0))
                def _():
                    emit(done, part, merged([here, take_back(OUTER, done, part)])[0])

                @pl.when((plane >= 1) & (upper == 1))
                def _():
                    emit(done, part, merged([here, take_back(OUTER, done, part), take_back(BESIDE, done, part)])[0])

        @pl.when((at >= 1) & (leaving < AH))
        def _():
            states = absorb([(load(leaving, part), part, ((2 * rows, rows, False),)) for part in wholes], leaving)
            for part, state in zip(wholes, states):
                store(leaving, part, state)
            arrived(NEAR, leaving, True)
            arrived(FAR, leaving, True)
            states = absorb([
                (load(leaving, part), part, ((rows, rows, False), (3 * rows, rows, False))) for part in wholes
            ], leaving)
            for part, (_, total, mixed) in zip(wholes, states):
                emit(leaving, part, mixed / total)

        @pl.when(entering < AH)
        def _():
            states = absorb([(None, part, (
                (part[0], rows - part[0], False), (WINDOW, part[0] + part[1], True)
            )) for part in halves], entering)
            for part, state in zip(halves, states):
                store(entering, part, state)

        @pl.when((at < moved) & (odd == 0))
        def _():
            own_part(at, WINDOW)

        @pl.when((at < moved) & (odd == 1))
        def _():
            own_part(at, WINDOW - rows)

        return carry

    lax.fori_loop(0, AH + 3, turn, 0)

    lax.fori_loop(AH + 3 - SETTLE_LAG, AH, finish, 0)

    @pl.when(me >= 4)
    def _():
        doc_copy(OUTER, doc_hbm, twin).wait_send()

    @pl.when((upper == 1) | jnp.logical_not(last))
    def _():
        doc_copy(BESIDE, doc_hbm, twin).wait_send()


def local(query_rows, key_rows, value_rows, doc_start, n):
    rows = query_rows.shape[0]
    reach = WINDOW // rows + 2
    operands = [
        pltpu.with_memory_space_constraint(x, pltpu.HBM)
        for x in (doc_start.reshape(1, rows), query_rows, key_rows, value_rows)
    ]
    mix, log = (2, AH, rows, DH), (2, AH, 2, rows)
    return pl.pallas_call(
        functools.partial(kernel, n, rows),
        out_shape=pltpu.VMEM(query_rows.shape, jnp.bfloat16),
        in_specs=[pl.BlockSpec(memory_space=pltpu.HBM)] * 4,
        out_specs=pl.BlockSpec(memory_space=pltpu.VMEM),
        scratch_shapes=[
            pltpu.VMEM((AH, rows, DH), jnp.bfloat16),
            pltpu.VMEM(mix, jnp.bfloat16),
            pltpu.VMEM((AH, reach * rows, DH), jnp.bfloat16),
            pltpu.VMEM((AH, reach * rows, DH), jnp.bfloat16),
            pltpu.VMEM((3, 1, rows), jnp.int32),
            pltpu.VMEM((3, rows, DH), jnp.int32),
            pltpu.VMEM((2, rows, DH), jnp.float32),
            pltpu.VMEM((2, rows, DH), jnp.float32),
            pltpu.VMEM((2, rows, DH), jnp.float32),
            pltpu.VMEM((AH, rows, DH), jnp.float32),
            pltpu.VMEM((AH, rows, DH), jnp.float32),
            pltpu.VMEM((4, rows, DH), jnp.float32),
            pltpu.VMEM((4, rows, DH), jnp.float32),
            pltpu.VMEM(mix, jnp.bfloat16),
            pltpu.VMEM(log, jnp.float32),
            pltpu.VMEM(mix, jnp.bfloat16),
            pltpu.VMEM(log, jnp.float32),
            pltpu.SemaphoreType.DMA,
            pltpu.SemaphoreType.DMA((2,)),
            pltpu.SemaphoreType.DMA((2,)),
            pltpu.SemaphoreType.DMA((5, AH)),
            pltpu.SemaphoreType.DMA((6, AH)),
            pltpu.SemaphoreType.DMA((PIECES,)),
        ],
        compiler_params=pltpu.CompilerParams(
            collective_id=0, has_side_effects=True, vmem_limit_bytes=56 * 1024 * 1024
        ),
    )(*operands)


def solution(mesh):
    placed = (
        P(("grp", "seq"), None),
        P(("grp", "seq"), None),
        P(("grp", "seq"), None),
        P(("grp", "seq")),
    )
    return jax.shard_map(
        functools.partial(local, n=mesh.shape["seq"]),
        mesh=mesh, in_specs=placed, out_specs=P(("grp", "seq"), None), check_vma=False,
    )
```
